128 devices in a mesh: expert: 8 (over z_lo, x), shard: 16 (over z_hi, y, core).
Axes of the slice: x: 4, y: 4, z: 4 (z_hi: 2, z_lo: 2; z = z_hi * 2 + z_lo), core: 2. Of those that a mesh axis runs over, the one named last changes fastest.
Arguments:
- grad_out: bfloat16 [8, 2048, 3072], P('expert', 'shard'), may hold values from -6 to 6
- gate_pre: bfloat16 [8, 2048, 8192], P('expert', None, 'shard'), may hold values from -8 to 8
- up_pre: bfloat16 [8, 2048, 8192], P('expert', None, 'shard'), may hold values from -6 to 6
- counts: int32 [8, 16], P('expert', 'shard'), may hold values from 32 to 128
- placement: int32 [8], replicated, may hold values from 0 to 63, as said below
- master: float32 [8, 8192, 3072], P('expert', 'shard')
Outputs:
- d_gate: bfloat16 [8, 2048, 8192], P('expert', None, 'shard')
- d_up: bfloat16 [8, 2048, 8192], P('expert', None, 'shard')
- new_master: float32 [8, 8192, 3072], P('expert', 'shard')
The draws below stay inside these ranges and needn't reach their ends.
Inputs may be any that keep to these rules, and one draw needn't show every extreme that they name: `placement`: slots that hold the same expert form aligned blocks of 1, 2 or 4 consecutive slots, each block starting at a multiple of its size; different blocks hold different experts.
All inputs are finite; a program needn't handle non-finite values.
Results may differ from the reference program's by a relative error of at most 0.006.
Values may be sent and summed in bfloat16 or wider, within the bound.
A program may use at most 256 MiB of HBM per device.

```python
import jax
import jax.numpy as jnp
from jax import lax

D = 3072
FFW = 8192
NEXP = 64
ROW_DEV = 128
SLOTS = 8
ROWS = 2048
N_SHARD = 16


def slot_experts(key):
    base = jax.random.fold_in(key, 3)
    patterns = jnp.array([[0, 0, 0, 0], [0, 0, 2, 2], [0, 0, 2, 3], [0, 1, 2, 2], [0, 1, 2, 3]], jnp.int32)
    blocks = SLOTS // 4
    picked = jax.random.randint(jax.random.fold_in(base, 1), (blocks,), 0, 5)
    leaders = patterns[picked] + 4 * jnp.arange(blocks, dtype=jnp.int32)[:, None]
    labels = jax.random.permutation(jax.random.fold_in(base, 2), NEXP - 1)[:SLOTS].astype(jnp.int32)
    top_block = jax.random.randint(jax.random.fold_in(base, 4), (), 0, blocks)
    labels = jnp.where(jnp.arange(SLOTS, dtype=jnp.int32) == 4 * top_block, NEXP - 1, labels).astype(jnp.int32)
    return labels[leaders.reshape(SLOTS)]


def draw_placement(key, part):
    return slot_experts(key)


def draw_master(key, part):
    labels = slot_experts(key)
    weight_key = jax.random.fold_in(key, 11)
    spread = jnp.float32(FFW) ** (-0.5)

    def one_slot(label):
        slot_key = jax.random.fold_in(weight_key, label)
        values = jax.random.normal(slot_key, (FFW, D), jnp.float32)
        return values * spread
    return jax.vmap(one_slot)(labels)


def set_ends(values, own_key, least, high):
    longest = values.shape.index(max(values.shape))
    spots = []
    for shift in (0, 1):
        where = [jax.random.randint(jax.random.fold_in(own_key, axis), (), 0, length) for axis, length in enumerate(values.shape)]
        where[longest] = (where[longest] + shift) % values.shape[longest]
        spots.append(tuple(where))
    return values.at[spots[0]].set(least).at[spots[1]].set(high)


def block_scale(rng, shape, split, low, high):
    def one(dim, parts):
        heights = jax.random.uniform(jax.random.fold_in(jax.random.fold_in(rng, 6), dim), (parts,), jnp.float32, low / len(split), high / len(split))
        return jnp.repeat(jnp.exp(heights), shape[dim] // parts).reshape((-1,) + (1,) * (len(shape) - dim - 1))

    loudness = one(*split[0])
    for cut in split[1:]:
        loudness = loudness * one(*cut)
    return loudness


def scatter_about(key, dims, deviation, bound, shards=(), held_as=jnp.bfloat16):
    level = block_scale(key, dims, shards, -0.22, 0.18) if shards else 1.0
    values = jax.random.normal(key, dims, jnp.float32) * deviation * level
    return jnp.minimum(jnp.maximum(values, -bound), bound).astype(held_as)


def setup_inputs(seed: int = 0) -> dict:
    splits = jax.random.split(jax.random.key(seed), 7)
    grad_out = scatter_about(splits[0], (SLOTS, ROWS, D), 1.0, 6.0, ((0, 8), (1, 16)))
    gate_pre = scatter_about(splits[1], (SLOTS, ROWS, FFW), 1.5, 8.0, ((0, 8), (2, 16)))
    up_pre = scatter_about(splits[2], (SLOTS, ROWS, FFW), 1.0, 6.0, ((0, 8), (2, 16)))
    counts = set_ends(jax.random.randint(splits[3], (SLOTS, N_SHARD), ROW_DEV // 4, ROW_DEV + 1), jax.random.fold_in(splits[3], 1), ROW_DEV // 4, ROW_DEV).astype(jnp.int32)
    placement = draw_placement(jax.random.fold_in(splits[6], 71), 0)
    master = draw_master(jax.random.fold_in(splits[6], 71), 0)
    return {"grad_out": grad_out, "gate_pre": gate_pre, "up_pre": up_pre, "counts": counts, "placement": placement, "master": master}


learn_rate = 0.02
rms_eps = 1e-06

def swiglu_back(out_grad, gate_pre, up_pre, master):
    weight_work = master.astype(jnp.bfloat16)
    gate_val = gate_pre.astype(jnp.float32)
    up_val = up_pre.astype(jnp.float32)
    gate_sig = jax.nn.sigmoid(gate_val)
    gate_act = gate_val * gate_sig
    d_hidden = lax.dot_general(out_grad, weight_work, (((1,), (1,)), ((), ())), preferred_element_type=jnp.float32)
    d_up = (d_hidden * gate_act).astype(jnp.bfloat16)
    d_gate = (d_hidden * up_val * (gate_sig * (1.0 + gate_val * (1.0 - gate_sig)))).astype(jnp.bfloat16)
    hidden = (gate_act * up_val).astype(jnp.bfloat16)
    weight_grad = lax.dot_general(hidden, out_grad, (((0,), (0,)), ((), ())), preferred_element_type=jnp.float32)
    return (d_gate, d_up, weight_grad)

def reference(grad_out, gate_pre, up_pre, counts, placement, master):
    row_pos = jnp.arange(ROWS, dtype=jnp.int32) % ROW_DEV
    limits = jnp.repeat(counts, ROW_DEV, axis=1)
    row_valid = (row_pos[None, :] < limits).astype(jnp.bfloat16)
    masked = grad_out * row_valid[:, :, None]
    d_gate, d_up, slot_grads = lax.map(lambda items: swiglu_back(*items), (masked, gate_pre, up_pre, master))

    def update(slot_index):
        partner_mask = (placement == placement[slot_index]).astype(jnp.float32)
        grad_sum = jnp.tensordot(partner_mask, slot_grads, axes=1, precision=lax.Precision.HIGHEST)
        row_rms = jnp.sqrt(lax.optimization_barrier(jnp.mean(grad_sum * grad_sum, axis=1, keepdims=True)) + rms_eps)
        return master[slot_index] - learn_rate * grad_sum / row_rms
    new_master = lax.map(update, jnp.arange(SLOTS, dtype=jnp.int32))
    return (d_gate, d_up, new_master)
```

```python
import jax
import jax.numpy as jnp
from jax import lax
from jax.sharding import PartitionSpec as P

learn_rate = 0.02
rms_eps = 1e-06
pieces = 6


def from_partner(shard, axis, flip):
    return lax.ppermute(shard, axis, [(i, i ^ flip) for i in range(lax.axis_size(axis))])


def per_device(grad_out, gate_pre, up_pre, counts, placement, master):
    weight_work = master[0].astype(jnp.bfloat16)
    local_rows, width = grad_out.shape[1], grad_out.shape[2]
    row_valid = (jnp.arange(local_rows, dtype=jnp.int32) < counts[0, 0]).astype(jnp.bfloat16)
    masked = grad_out[0] * row_valid[:, None]
    gate_val = gate_pre[0].astype(jnp.float32)
    up_val = up_pre[0].astype(jnp.float32)
    gate_sig = jax.nn.sigmoid(gate_val)
    gate_act = gate_val * gate_sig
    gate_slope = gate_sig * (1.0 + gate_val * (1.0 - gate_sig))
    hidden = (gate_act * up_val).astype(jnp.bfloat16)
    my_slot = lax.axis_index("expert")
    slot_order = jnp.arange(placement.shape[0], dtype=jnp.int32)

    def expert_of(slot):
        return jnp.sum(jnp.where(slot_order == slot, placement, 0))

    my_expert = expert_of(my_slot)
    same_pair = my_expert == expert_of(my_slot ^ 1)
    same_quad = my_expert == expert_of(my_slot ^ 3)
    step = width // pieces
    d_hidden = 0.0
    sums = []
    for piece in range(pieces):
        cols = slice(piece * step, (piece + 1) * step)
        rows = lax.all_gather(masked[:, cols], "shard", axis=0, tiled=True)
        grad = lax.dot_general(
            hidden, rows, (((0,), (0,)), ((), ())), preferred_element_type=jnp.float32
        )
        for flip, same in ((1, same_pair), (3, same_quad)):
            received = from_partner(grad.astype(jnp.bfloat16), "expert", flip)
            grad = grad + jnp.where(same, received.astype(jnp.float32), 0.0)
        sums.append(grad)
        d_hidden = d_hidden + lax.dot_general(
            rows, weight_work[:, cols], (((1,), (1,)), ((), ())), preferred_element_type=jnp.float32
        )
    up_acc = (d_hidden * gate_act).astype(jnp.bfloat16)
    gate_acc = (d_hidden * up_val * gate_slope).astype(jnp.bfloat16)
    grad_sum = jnp.concatenate(sums, axis=1)
    row_rms = jnp.sqrt(jnp.mean(grad_sum * grad_sum, axis=1, keepdims=True) + rms_eps)
    new_master = master[0] - learn_rate * grad_sum / row_rms
    return (gate_acc[None], up_acc[None], new_master[None])


def solution(mesh):
    return jax.shard_map(
        per_device,
        mesh=mesh,
        in_specs=(
            P("expert", "shard", None),
            P("expert", None, "shard"),
            P("expert", None, "shard"),
            P("expert", "shard"),
            P(),
            P("expert", "shard", None),
        ),
        out_specs=(
            P("expert", None, "shard"),
            P("expert", None, "shard"),
            P("expert", "shard", None),
        ),
        check_vma=False,
    )
```

```python
import jax
import jax.numpy as jnp
from jax import lax
from jax.experimental import pallas as pl
from jax.experimental.pallas import tpu as pltpu
from jax.sharding import PartitionSpec as P

learn_rate = 0.02
rms_eps = 1e-06
chunk = 256
row_tile = 256
out_tile = 64
MESH = pl.DeviceIdType.MESH


def activations(gate_ref, up_ref, rows):
    gate_val = gate_ref[rows, :].astype(jnp.float32)
    up_val = up_ref[rows, :].astype(jnp.float32)
    return gate_val, up_val, lax.logistic(gate_val)


def kernel(
    grad_hbm, gate_hbm, up_hbm, counts_ref, place_ref, master_hbm,
    dgate_hbm, dup_hbm, new_hbm,
    grad_v, rows_v, gate_v, up_v, hidden_t, d_hidden, weight_v, master_v, total,
    pair_out, pair_in, quad_out, quad_in, squares,
    load_sem, store_sem, gather_send, gather_recv, pair_send, pair_recv, quad_send, quad_recv,
):
    expert, shard = lax.axis_index("expert"), lax.axis_index("shard")
    block, width = grad_v.shape
    n_chunks = width // chunk
    n_rows, n_hidden = gate_v.shape
    half = n_hidden // 2
    n_tiles = n_rows // row_tile

    core = shard % 2
    y = (shard // 2) % 4
    z_base = (shard // 8) * 8
    z_other = (z_base + 8) % 16

    def at(base, step):
        return base + ((y + step + 4) % 4) * 2 + core

    up_id, down_id, far_id = at(z_base, 1), at(z_base, -1), at(z_base, 2)
    across_id = at(z_other, 0)
    sibling_id = shard + 1 - 2 * core
    way = 1 - 2 * core
    pair_id = expert + 1 - 2 * (expert % 2)
    quad_id = expert + 3 - 2 * (expert % 4)

    barrier = pltpu.get_barrier_semaphore()
    for peer in (
        (expert, up_id), (expert, down_id), (expert, across_id), (expert, sibling_id),
        (pair_id, shard), (quad_id, shard),
    ):
        pl.semaphore_signal(barrier, inc=1, device_id=peer, device_id_type=MESH)

    def load(src, dst, index):
        return pltpu.make_async_copy(src, dst, load_sem.at[index])

    quarter = n_rows // 4

    def gate_load(part):
        rows = pl.ds(pl.multiple_of(part * quarter, quarter), quarter)
        return load(gate_hbm.at[rows], gate_v.at[rows], 2 + part)

    def up_load(part):
        rows = pl.ds(pl.multiple_of(part * quarter, quarter), quarter)
        return load(up_hbm.at[rows], up_v.at[rows], 6 + part)

    grad_load = load(grad_hbm, grad_v, 0)
    master_load = load(master_hbm, master_v, 1)
    grad_load.start()
    for part in range(4):
        gate_load(part).start()
        up_load(part).start()
    master_load.start()

    same_pair = jnp.where(place_ref[expert] == place_ref[pair_id], 1.0, 0.0)
    same_quad = jnp.where(place_ref[expert] == place_ref[quad_id], 1.0, 0.0)

    def rows_of(c, b):
        return rows_v.at[c, pl.ds(pl.multiple_of(b * block, block), block)]

    def some_blocks(c, n):
        return rows_v.at[c, pl.ds(0, n * block)]

    def push(c, b, target, stage):
        pltpu.make_async_remote_copy(
            src_ref=rows_of(c, b),
            dst_ref=rows_of(c, b),
            send_sem=gather_send.at[c],
            recv_sem=gather_recv.at[c, stage],
            device_id=(expert, target),
            device_id_type=MESH,
        ).start()

    def arrived(c, stage, n):
        pltpu.make_async_copy(
            some_blocks(c, n), some_blocks(c, n), gather_recv.at[c, stage]
        ).wait()

    def exchange(out, landing, send_sem, recv_sem, target, c, h):
        return pltpu.make_async_remote_copy(
            src_ref=out.at[c, h],
            dst_ref=landing.at[c, h],
            send_sem=send_sem.at[c, h],
            recv_sem=recv_sem.at[c, h],
            device_id=(target, shard),
            device_id_type=MESH,
        )

    def pair_copy(c, h):
        return exchange(pair_out, pair_in, pair_send, pair_recv, pair_id, c, h)

    def quad_copy(c, h):
        return exchange(quad_out, quad_in, quad_send, quad_recv, quad_id, c, h)

    def columns(c):
        return pl.ds(pl.multiple_of(c * chunk, chunk), chunk)

    grad_load.wait()
    live = lax.broadcasted_iota(jnp.int32, (block, chunk), 0) < counts_ref[0, 0]
    own_rows = pl.ds(pl.multiple_of(shard * block, block), block)

    @pl.loop(0, n_chunks)
    def _(c):
        values = grad_v[:, columns(c)].astype(jnp.float32)
        rows_v[c, own_rows, :] = jnp.where(live, values, 0.0).astype(jnp.bfloat16)

    pl.semaphore_wait(barrier, 6)

    def make_hidden(tile):
        rows = pl.ds(pl.multiple_of(tile * row_tile, row_tile), row_tile)
        gate_val, up_val, sig = activations(gate_v, up_v, rows)
        hidden_t[:, rows] = jnp.transpose(gate_val * sig * up_val).astype(jnp.bfloat16)

    def finish_rows(tile):
        rows = pl.ds(pl.multiple_of(tile * row_tile, row_tile), row_tile)
        gate_val, up_val, sig = activations(gate_v, up_v, rows)
        grad = d_hidden[rows, :]
        up_v[rows, :] = (grad * (gate_val * sig)).astype(jnp.bfloat16)
        slope = sig * (1.0 + gate_val * (1.0 - sig))
        gate_v[rows, :] = (grad * up_val * slope).astype(jnp.bfloat16)
        pltpu.make_async_copy(gate_v.at[rows], dgate_hbm.at[rows], store_sem.at[0, tile]).start()
        pltpu.make_async_copy(up_v.at[rows], dup_hbm.at[rows], store_sem.at[1, tile]).start()

    def step(t, carry):
        @pl.when(t < n_chunks)
        def _():
            for target in (up_id, down_id, across_id):
                push(t, shard, target, 0)
            push(t, shard, sibling_id, 3)

        @pl.when(jnp.logical_and(t >= 1, t < n_chunks + 1))
        def _():
            c = t - 1
            arrived(c, 0, 3)
            push(c, across_id, up_id, 1)
            push(c, across_id, down_id, 1)
            push(c, at(z_base, -way), at(z_base, way), 1)
            for b in (across_id, up_id, down_id):
                push(c, b, sibling_id, 3)

        @pl.when(jnp.logical_and(t >= 2, t < n_chunks + 2))
        def _():
            c = t - 2
            arrived(c, 1, 3)
            push(c, far_id, across_id, 2)
            for b in (far_id, at(z_other, 1), at(z_other, -1)):
                push(c, b, sibling_id, 3)

        @pl.when(jnp.logical_and(t >= 3, t < n_chunks + 3))
        def _():
            c = t - 3
            arrived(c, 2, 1)
            push(c, at(z_other, 2), sibling_id, 3)

        @pl.when(t < 4)
        def _():
            gate_load(t).wait()
            up_load(t).wait()
            for k in range(2):
                make_hidden(2 * t + k)

        @pl.when(t == 3)
        def _():
            master_load.wait()
            d_hidden[...] = jnp.zeros_like(d_hidden)
            squares[...] = jnp.zeros_like(squares)

        @pl.when(jnp.logical_and(t >= 4, t < n_chunks + 4))
        def _():
            c = t - 4
            arrived(c, 3, 8)
            for h in range(2):
                part = pl.ds(h * half, half)
                grad = jnp.dot(
                    hidden_t[part, :], rows_v[c], preferred_element_type=jnp.float32
                )
                total[part, columns(c)] = grad
                pair_out[c, h] = grad.astype(jnp.bfloat16)
                pair_copy(c, h).start()
            weight_v[...] = master_v[:, columns(c)].astype(jnp.bfloat16)

            @pl.loop(0, n_tiles)
            def _(tile):
                rows = pl.ds(pl.multiple_of(tile * row_tile, row_tile), row_tile)
                d_hidden[rows, :] += lax.dot_general(
                    rows_v[c, rows, :], weight_v[...], (((1,), (1,)), ((), ())),
                    preferred_element_type=jnp.float32,
                )

        @pl.when(jnp.logical_and(t >= 5, t < n_chunks + 5))
        def _():
            c = t - 5
            for h in range(2):
                part = pl.ds(h * half, half)
                pair_copy(c, h).wait_recv()
                both = total[part, columns(c)] + same_pair * pair_in[c, h].astype(jnp.float32)
                total[part, columns(c)] = both
                quad_out[c, h] = both.astype(jnp.bfloat16)
                quad_copy(c, h).start()

        @pl.when(jnp.logical_and(t >= n_chunks + 3, t < n_chunks + 5))
        def _():
            @pl.loop(0, n_tiles // 2)
            def _(k):
                finish_rows((t - n_chunks - 3) * (n_tiles // 2) + k)

        @pl.when(t >= 7)
        def _():
            c = t - 7
            for h in range(2):
                part = pl.ds(h * half, half)
                quad_copy(c, h).wait_recv()
                whole = total[part, columns(c)] + same_quad * quad_in[c, h].astype(jnp.float32)
                total[part, columns(c)] = whole
                square = whole * whole
                squares[part, :] += square[:, :128] + square[:, 128:]

        return carry

    lax.fori_loop(0, n_chunks + 7, step, 0)

    def new_store(tile):
        rows = pl.ds(pl.multiple_of(tile * out_tile, out_tile), out_tile)
        return pltpu.make_async_copy(master_v.at[rows], new_hbm.at[rows], store_sem.at[2, tile])

    @pl.loop(0, n_hidden // out_tile)
    def _(tile):
        rows = pl.ds(pl.multiple_of(tile * out_tile, out_tile), out_tile)
        mean = jnp.sum(squares[rows, :], axis=1, keepdims=True) / width
        scale = learn_rate / jnp.sqrt(mean + rms_eps)
        master_v[rows, :] = master_v[rows, :] - total[rows, :] * scale
        new_store(tile).start()

    @pl.loop(0, n_chunks)
    def _(c):
        pltpu.make_async_copy(some_blocks(c, 15), some_blocks(c, 15), gather_send.at[c]).wait()
        for h in range(2):
            pair_copy(c, h).wait_send()
            quad_copy(c, h).wait_send()

    @pl.loop(0, n_tiles)
    def _(tile):
        rows = pl.ds(pl.multiple_of(tile * row_tile, row_tile), row_tile)
        pltpu.make_async_copy(gate_v.at[rows], dgate_hbm.at[rows], store_sem.at[0, tile]).wait()
        pltpu.make_async_copy(up_v.at[rows], dup_hbm.at[rows], store_sem.at[1, tile]).wait()

    @pl.loop(0, n_hidden // out_tile)
    def _(tile):
        new_store(tile).wait()


def per_device(grad_out, gate_pre, up_pre, counts, placement, master):
    block, width = grad_out.shape[1:]
    n_rows, n_hidden = gate_pre.shape[1:]
    n_chunks = width // chunk
    half = n_hidden // 2
    hbm = pl.BlockSpec(memory_space=pl.ANY)
    smem = pl.BlockSpec(memory_space=pltpu.SMEM)
    dma = pltpu.SemaphoreType.DMA
    pieces = (n_chunks, 2, half, chunk)
    d_gate, d_up, new_master = pl.pallas_call(
        kernel,
        out_shape=(
            jax.ShapeDtypeStruct((n_rows, n_hidden), jnp.bfloat16),
            jax.ShapeDtypeStruct((n_rows, n_hidden), jnp.bfloat16),
            jax.ShapeDtypeStruct((n_hidden, width), jnp.float32),
        ),
        in_specs=[hbm, hbm, hbm, smem, smem, hbm],
        out_specs=(hbm, hbm, hbm),
        scratch_shapes=[
            pltpu.VMEM((block, width), jnp.bfloat16),
            pltpu.VMEM((n_chunks, n_rows, chunk), jnp.bfloat16),
            pltpu.VMEM((n_rows, n_hidden), jnp.bfloat16),
            pltpu.VMEM((n_rows, n_hidden), jnp.bfloat16),
            pltpu.VMEM((n_hidden, n_rows), jnp.bfloat16),
            pltpu.VMEM((n_rows, n_hidden), jnp.float32),
            pltpu.VMEM((n_hidden, chunk), jnp.bfloat16),
            pltpu.VMEM((n_hidden, width), jnp.float32),
            pltpu.VMEM((n_hidden, width), jnp.float32),
            pltpu.VMEM(pieces, jnp.bfloat16),
            pltpu.VMEM(pieces, jnp.bfloat16),
            pltpu.VMEM(pieces, jnp.bfloat16),
            pltpu.VMEM(pieces, jnp.bfloat16),
            pltpu.VMEM((n_hidden, 128), jnp.float32),
            dma((10,)),
            dma((3, 8)),
            dma((n_chunks,)),
            dma((n_chunks, 4)),
            dma((n_chunks, 2)),
            dma((n_chunks, 2)),
            dma((n_chunks, 2)),
            dma((n_chunks, 2)),
        ],
        compiler_params=pltpu.CompilerParams(
            collective_id=0, has_side_effects=True, vmem_limit_bytes=58 * 2**20
        ),
    )(grad_out[0], gate_pre[0], up_pre[0], counts, placement, master[0])
    return d_gate[None], d_up[None], new_master[None]


def solution(mesh):
    return jax.shard_map(
        per_device,
        mesh=mesh,
        in_specs=(
            P("expert", "shard", None),
            P("expert", None, "shard"),
            P("expert", None, "shard"),
            P("expert", "shard"),
            P(),
            P("expert", "shard", None),
        ),
        out_specs=(
            P("expert", None, "shard"),
            P("expert", None, "shard"),
            P("expert", "shard", None),
        ),
        check_vma=False,
    )
```

```python
import jax
import jax.numpy as jnp
from jax import lax
from jax.experimental import pallas as pl
from jax.experimental.pallas import tpu as pltpu
from jax.sharding import PartitionSpec as P

learn_rate = 0.02
rms_eps = 1e-06
piece = 128
chunk = 256
row_tile = 256
out_tile = 64
MESH = pl.DeviceIdType.MESH


def activations(gate_ref, up_ref, rows):
    gate_val = gate_ref[rows, :].astype(jnp.float32)
    up_val = up_ref[rows, :].astype(jnp.float32)
    return gate_val, up_val, lax.logistic(gate_val)


def kernel(
    grad_hbm, gate_hbm, up_hbm, counts_ref, place_ref, master_hbm,
    gate_v, up_v, master_v, total, squares,
    grad_v, rows_v, hidden_t, d_hidden, weight_t,
    pair_out, pair_in, quad_out, quad_in,
    load_sem, gather_send, gather_recv, pair_send, pair_recv, quad_send, quad_recv,
):
    expert, shard = lax.axis_index("expert"), lax.axis_index("shard")
    block, width = grad_v.shape
    n_pieces = width // piece
    n_units = n_pieces // 2 + 1
    n_rows, n_hidden = gate_v.shape
    n_tiles = n_rows // row_tile

    core = shard % 2
    y = (shard // 2) % 4
    z_base = (shard // 8) * 8
    z_other = (z_base + 8) % 16

    def at(base, step):
        return base + ((y + step + 4) % 4) * 2 + core

    up_id, down_id, far_id = at(z_base, 1), at(z_base, -1), at(z_base, 2)
    across_id = at(z_other, 0)
    sibling_id = shard + 1 - 2 * core
    way = 1 - 2 * core
    pair_id = expert + 1 - 2 * (expert % 2)
    quad_id = expert + 3 - 2 * (expert % 4)

    barrier = pltpu.get_barrier_semaphore()
    for peer in (
        (expert, up_id), (expert, down_id), (expert, across_id), (expert, sibling_id),
        (pair_id, shard), (quad_id, shard),
    ):
        pl.semaphore_signal(barrier, inc=1, device_id=peer, device_id_type=MESH)

    def load(src, dst, index):
        return pltpu.make_async_copy(src, dst, load_sem.at[index])

    quarter = n_rows // 4

    def gate_load(part):
        rows = pl.ds(pl.multiple_of(part * quarter, quarter), quarter)
        return load(gate_hbm.at[rows], gate_v.at[rows], 3 + part)

    def up_load(part):
        rows = pl.ds(pl.multiple_of(part * quarter, quarter), quarter)
        return load(up_hbm.at[rows], up_v.at[rows], 7 + part)

    first, rest = pl.ds(0, chunk), pl.ds(chunk, width - chunk)
    first_load = load(grad_hbm.at[:, first], grad_v.at[:, first], 0)
    rest_load = load(grad_hbm.at[:, rest], grad_v.at[:, rest], 1)
    master_load = load(master_hbm, master_v, 2)
    first_load.start()
    for part in range(4):
        gate_load(part).start()
        up_load(part).start()
    rest_load.start()
    master_load.start()

    same_pair = jnp.where(place_ref[expert] == place_ref[pair_id], 1.0, 0.0)
    same_quad = jnp.where(place_ref[expert] == place_ref[quad_id], 1.0, 0.0)

    def block_of(p, n, b):
        return rows_v.at[pl.ds(p, n), pl.ds(pl.multiple_of(b * block, block), block)]

    def some_blocks(n, k):
        return rows_v.at[pl.ds(0, n), pl.ds(0, k * block)]

    def per_unit(u, act):
        @pl.when(u < 2)
        def _():
            act(u, 1)

        @pl.when(u >= 2)
        def _():
            act(2 * u - 2, 2)

    def push(u, p, n, b, target, stage):
        pltpu.make_async_remote_copy(
            src_ref=block_of(p, n, b),
            dst_ref=block_of(p, n, b),
            send_sem=gather_send.at[u],
            recv_sem=gather_recv.at[u, stage],
            device_id=(expert, target),
            device_id_type=MESH,
        ).start()

    def arrived(u, n, stage, k):
        blocks = some_blocks(n, k)
        pltpu.make_async_copy(blocks, blocks, gather_recv.at[u, stage]).wait()

    def exchange(out, landing, send_sem, recv_sem, target, p):
        return pltpu.make_async_remote_copy(
            src_ref=out.at[p],
            dst_ref=landing.at[p],
            send_sem=send_sem.at[p],
            recv_sem=recv_sem.at[p],
            device_id=(target, shard),
            device_id_type=MESH,
        )

    def pair_copy(p):
        return exchange(pair_out, pair_in, pair_send, pair_recv, pair_id, p)

    def quad_copy(p):
        return exchange(quad_out, quad_in, quad_send, quad_recv, quad_id, p)

    def columns(p, n):
        return pl.ds(pl.multiple_of(p * piece, piece), n * piece)

    def rows_of(p, n):
        if n == 1:
            return rows_v[p]
        return jnp.concatenate([rows_v[p], rows_v[p + 1]], axis=1)

    live = lax.broadcasted_iota(jnp.int32, (block, piece), 0) < counts_ref[0, 0]
    own_rows = pl.ds(pl.multiple_of(shard * block, block), block)

    def mask_piece(p):
        values = grad_v[:, columns(p, 1)].astype(jnp.float32)
        rows_v[p, own_rows, :] = jnp.where(live, values, 0.0).astype(jnp.bfloat16)

    first_load.wait()
    mask_piece(0)
    mask_piece(1)
    pl.semaphore_wait(barrier, 6)

    def make_hidden(tile):
        rows = pl.ds(pl.multiple_of(tile * row_tile, row_tile), row_tile)
        gate_val, up_val, sig = activations(gate_v, up_v, rows)
        hidden_t[:, rows] = jnp.transpose(gate_val * sig * up_val).astype(jnp.bfloat16)

    def finish_rows(tile):
        rows = pl.ds(pl.multiple_of(tile * row_tile, row_tile), row_tile)
        gate_val, up_val, sig = activations(gate_v, up_v, rows)
        grad = d_hidden[rows, :]
        up_v[rows, :] = (grad * (gate_val * sig)).astype(jnp.bfloat16)
        slope = sig * (1.0 + gate_val * (1.0 - sig))
        gate_v[rows, :] = (grad * up_val * slope).astype(jnp.bfloat16)

    def during(t, delay, body):
        @pl.when(jnp.logical_and(t >= delay, t < n_units + delay))
        def _():
            body(t - delay)

    def step(t, carry):
        def weight_grad(u):
            def act(p, n):
                arrived(u, n, 3, 8)
                grad = jnp.dot(hidden_t[...], rows_of(p, n), preferred_element_type=jnp.float32)
                total[:, columns(p, n)] = grad
                for k in range(n):
                    pair_out[p + k] = grad[:, k * piece : (k + 1) * piece].astype(jnp.bfloat16)
                    pair_copy(p + k).start()

            per_unit(u, act)

        def stage_three(u):
            def act(p, n):
                arrived(u, n, 2, 1)
                push(u, p, n, at(z_other, 2), sibling_id, 3)

            per_unit(u, act)

        def stage_two(u):
            def act(p, n):
                arrived(u, n, 1, 3)
                push(u, p, n, far_id, across_id, 2)
                for b in (far_id, at(z_other, 1), at(z_other, -1)):
                    push(u, p, n, b, sibling_id, 3)

            per_unit(u, act)

        def stage_one(u):
            def act(p, n):
                arrived(u, n, 0, 3)
                push(u, p, n, across_id, up_id, 1)
                push(u, p, n, across_id, down_id, 1)
                push(u, p, n, at(z_base, -way), at(z_base, way), 1)
                for b in (across_id, up_id, down_id):
                    push(u, p, n, b, sibling_id, 3)

            per_unit(u, act)

        def stage_zero(u):
            def act(p, n):
                for target in (across_id, up_id, down_id):
                    push(u, p, n, shard, target, 0)
                push(u, p, n, shard, sibling_id, 3)

            per_unit(u, act)

        def data_grad(u):
            @pl.when(u >= 1)
            def _():
                p = 2 * u - 2
                weight_t[...] = jnp.transpose(master_v[:, columns(p, 2)]).astype(jnp.bfloat16)
                d_hidden[...] += jnp.dot(
                    rows_of(p, 2), weight_t[...], preferred_element_type=jnp.float32
                )

        def pair_sum(u):
            def act(p, n):
                for k in range(n):
                    pair_copy(p + k).wait_recv()
                    part = columns(p + k, 1)
                    both = total[:, part] + same_pair * pair_in[p + k].astype(jnp.float32)
                    total[:, part] = both
                    quad_out[p + k] = both.astype(jnp.bfloat16)
                    quad_copy(p + k).start()

            per_unit(u, act)

        def quad_sum(u):
            def act(p, n):
                for k in range(n):
                    quad_copy(p + k).wait_recv()
                    part = columns(p + k, 1)
                    whole = total[:, part] + same_quad * quad_in[p + k].astype(jnp.float32)
                    total[:, part] = whole
                    squares[...] += whole * whole

            per_unit(u, act)

        during(t, 4, weight_grad)
        during(t, 3, stage_three)
        during(t, 2, stage_two)
        during(t, 1, stage_one)
        during(t, 0, stage_zero)

        @pl.when(t < 4)
        def _():
            gate_load(t).wait()
            up_load(t).wait()
            for k in range(2):
                make_hidden(2 * t + k)

        @pl.when(t == 1)
        def _():
            rest_load.wait()

            @pl.loop(2, n_pieces)
            def _(p):
                mask_piece(p)

        @pl.when(t == 4)
        def _():
            master_load.wait()
            d_hidden[...] = jnp.zeros_like(d_hidden)
            squares[...] = jnp.zeros_like(squares)

        during(t, 4, data_grad)
        during(t, 5, pair_sum)

        @pl.when(jnp.logical_and(t >= n_units + 3, t < n_units + 5))
        def _():
            @pl.loop(0, n_tiles // 2)
            def _(k):
                finish_rows((t - n_units - 3) * (n_tiles // 2) + k)

        during(t, 7, quad_sum)
        return carry

    lax.fori_loop(0, n_units + 7, step, 0)

    @pl.loop(0, n_units)
    def _(u):
        def act(p, n):
            blocks = some_blocks(n, 15)
            pltpu.make_async_copy(blocks, blocks, gather_send.at[u]).wait()
            for k in range(n):
                pair_copy(p + k).wait_send()
                quad_copy(p + k).wait_send()

        per_unit(u, act)


def finish(
    gate_v, up_v, master_v, total, squares, dgate_hbm, dup_hbm, new_hbm, new_v, store_sem
):
    n_rows, (n_hidden, width) = gate_v.shape[0], master_v.shape
    parts = 4
    copies = []
    for index, (src, dst) in enumerate(((gate_v, dgate_hbm), (up_v, dup_hbm))):
        for part in range(parts):
            rows = pl.ds(part * (n_rows // parts), n_rows // parts)
            copies.append(
                pltpu.make_async_copy(src.at[rows], dst.at[rows], store_sem.at[index, part])
            )

    def new_store(tile):
        rows = pl.ds(pl.multiple_of(tile * out_tile, out_tile), out_tile)
        return pltpu.make_async_copy(new_v.at[rows], new_hbm.at[rows], store_sem.at[2, tile])

    for copy in copies:
        copy.start()

    @pl.loop(0, n_hidden // out_tile)
    def _(tile):
        rows = pl.ds(pl.multiple_of(tile * out_tile, out_tile), out_tile)
        mean = jnp.sum(squares[rows, :], axis=1, keepdims=True) / width
        scale = learn_rate / jnp.sqrt(mean + rms_eps)
        new_v[rows, :] = master_v[rows, :] - total[rows, :] * scale
        new_store(tile).start()

    for copy in copies:
        copy.wait()

    @pl.loop(0, n_hidden // out_tile)
    def _(tile):
        new_store(tile).wait()


def per_device(grad_out, gate_pre, up_pre, counts, placement, master):
    block, width = grad_out.shape[1:]
    n_rows, n_hidden = gate_pre.shape[1:]
    n_pieces = width // piece
    n_units = n_pieces // 2 + 1
    hbm = pl.BlockSpec(memory_space=pl.ANY)
    smem = pl.BlockSpec(memory_space=pltpu.SMEM)
    vmem = pl.BlockSpec(memory_space=pltpu.VMEM)
    dma = pltpu.SemaphoreType.DMA
    pieces = (n_pieces, n_hidden, piece)
    held = pl.pallas_call(
        kernel,
        out_shape=(
            pltpu.VMEM((n_rows, n_hidden), jnp.bfloat16),
            pltpu.VMEM((n_rows, n_hidden), jnp.bfloat16),
            pltpu.VMEM((n_hidden, width), jnp.float32),
            pltpu.VMEM((n_hidden, width), jnp.float32),
            pltpu.VMEM((n_hidden, piece), jnp.float32),
        ),
        in_specs=[hbm, hbm, hbm, smem, smem, hbm],
        out_specs=(vmem,) * 5,
        scratch_shapes=[
            pltpu.VMEM((block, width), jnp.bfloat16),
            pltpu.VMEM((n_pieces, n_rows, piece), jnp.bfloat16),
            pltpu.VMEM((n_hidden, n_rows), jnp.bfloat16),
            pltpu.VMEM((n_rows, n_hidden), jnp.float32),
            pltpu.VMEM((chunk, n_hidden), jnp.bfloat16),
            pltpu.VMEM(pieces, jnp.bfloat16),
            pltpu.VMEM(pieces, jnp.bfloat16),
            pltpu.VMEM(pieces, jnp.bfloat16),
            pltpu.VMEM(pieces, jnp.bfloat16),
            dma((11,)),
            dma((n_units,)),
            dma((n_units, 4)),
            dma((n_pieces,)),
            dma((n_pieces,)),
            dma((n_pieces,)),
            dma((n_pieces,)),
        ],
        compiler_params=pltpu.CompilerParams(
            collective_id=0, has_side_effects=True, vmem_limit_bytes=40 * 2**20
        ),
    )(grad_out[0], gate_pre[0], up_pre[0], counts, placement, master[0])
    d_gate, d_up, new_master = pl.pallas_call(
        finish,
        out_shape=(
            jax.ShapeDtypeStruct((n_rows, n_hidden), jnp.bfloat16),
            jax.ShapeDtypeStruct((n_rows, n_hidden), jnp.bfloat16),
            jax.ShapeDtypeStruct((n_hidden, width), jnp.float32),
        ),
        in_specs=[vmem] * 5,
        out_specs=(hbm,) * 3,
        scratch_shapes=[pltpu.VMEM((n_hidden, width), jnp.float32), dma((3, 8))],
        compiler_params=pltpu.CompilerParams(vmem_limit_bytes=20 * 2**20),
    )(*held)
    return d_gate[None], d_up[None], new_master[None]


def solution(mesh):
    return jax.shard_map(
        per_device,
        mesh=mesh,
        in_specs=(
            P("expert", "shard", None),
            P("expert", None, "shard"),
            P("expert", None, "shard"),
            P("expert", "shard"),
            P(),
            P("expert", "shard", None),
        ),
        out_specs=(
            P("expert", None, "shard"),
            P("expert", None, "shard"),
            P("expert", "shard", None),
        ),
        check_vma=False,
    )
```

```python
import jax
import jax.numpy as jnp
from jax import lax
from jax.experimental import pallas as pl
from jax.experimental.pallas import tpu as pltpu
from jax.sharding import PartitionSpec as P

learn_rate = 0.02
rms_eps = 1e-06
piece = 128
chunk = 256
row_tile = 256
out_tile = 64
MESH = pl.DeviceIdType.MESH


def activations(gate_ref, up_ref, rows):
    gate_val = gate_ref[rows, :].astype(jnp.float32)
    up_val = up_ref[rows, :].astype(jnp.float32)
    return gate_val, up_val, lax.logistic(gate_val)


def kernel(
    grad_hbm, gate_hbm, up_hbm, counts_ref, place_ref, master_hbm,
    gate_v, up_v, master_v, total, squares,
    grad_v, rows_v, hidden_t, d_hidden, weight_t,
    pair_out, pair_in, quad_out, quad_in,
    load_sem, gather_send, gather_recv, pair_send, pair_recv, quad_send, quad_recv,
):
    expert, shard = lax.axis_index("expert"), lax.axis_index("shard")
    block, width = grad_v.shape
    n_pieces = width // piece
    n_units = n_pieces // 2 + 1
    n_rows, n_hidden = gate_v.shape
    n_tiles = n_rows // row_tile

    core = shard % 2
    y = (shard // 2) % 4
    z_base = (shard // 8) * 8
    z_other = (z_base + 8) % 16

    def at(base, step):
        return base + ((y + step + 4) % 4) * 2 + core

    up_id, down_id, far_id = at(z_base, 1), at(z_base, -1), at(z_base, 2)
    across_id = at(z_other, 0)
    sibling_id = shard + 1 - 2 * core
    way = 1 - 2 * core
    pair_id = expert + 1 - 2 * (expert % 2)
    quad_id = expert + 3 - 2 * (expert % 4)

    barrier = pltpu.get_barrier_semaphore()
    for peer in (
        (expert, up_id), (expert, down_id), (expert, far_id), (expert, across_id),
        (expert, sibling_id), (pair_id, shard), (quad_id, shard),
    ):
        pl.semaphore_signal(barrier, inc=1, device_id=peer, device_id_type=MESH)

    def load(src, dst, index):
        return pltpu.make_async_copy(src, dst, load_sem.at[index])

    quarter = n_rows // 4

    def gate_load(part):
        rows = pl.ds(pl.multiple_of(part * quarter, quarter), quarter)
        return load(gate_hbm.at[rows], gate_v.at[rows], 3 + part)

    def up_load(part):
        rows = pl.ds(pl.multiple_of(part * quarter, quarter), quarter)
        return load(up_hbm.at[rows], up_v.at[rows], 7 + part)

    first, rest = pl.ds(0, chunk), pl.ds(chunk, width - chunk)
    first_load = load(grad_hbm.at[:, first], grad_v.at[:, first], 0)
    rest_load = load(grad_hbm.at[:, rest], grad_v.at[:, rest], 1)
    master_load = load(master_hbm, master_v, 2)
    first_load.start()
    for part in range(4):
        gate_load(part).start()
        up_load(part).start()
    rest_load.start()
    master_load.start()

    same_pair = jnp.where(place_ref[expert] == place_ref[pair_id], 1.0, 0.0)
    same_quad = jnp.where(place_ref[expert] == place_ref[quad_id], 1.0, 0.0)

    def block_of(p, n, b):
        return rows_v.at[pl.ds(p, n), pl.ds(pl.multiple_of(b * block, block), block)]

    def some_blocks(n, k):
        return rows_v.at[pl.ds(0, n), pl.ds(0, k * block)]

    def per_unit(u, act):
        @pl.when(u < 2)
        def _():
            act(u, 1)

        @pl.when(u >= 2)
        def _():
            act(2 * u - 2, 2)

    def push(u, p, n, b, target, stage):
        pltpu.make_async_remote_copy(
            src_ref=block_of(p, n, b),
            dst_ref=block_of(p, n, b),
            send_sem=gather_send.at[u],
            recv_sem=gather_recv.at[u, stage],
            device_id=(expert, target),
            device_id_type=MESH,
        ).start()

    def arrived(u, n, stage, k):
        blocks = some_blocks(n, k)
        pltpu.make_async_copy(blocks, blocks, gather_recv.at[u, stage]).wait()

    def exchange(out, landing, send_sem, recv_sem, target, p):
        return pltpu.make_async_remote_copy(
            src_ref=out.at[p],
            dst_ref=landing.at[p],
            send_sem=send_sem.at[p],
            recv_sem=recv_sem.at[p],
            device_id=(target, shard),
            device_id_type=MESH,
        )

    def pair_copy(p):
        return exchange(pair_out, pair_in, pair_send, pair_recv, pair_id, p)

    def quad_copy(p):
        return exchange(quad_out, quad_in, quad_send, quad_recv, quad_id, p)

    def columns(p, n):
        return pl.ds(pl.multiple_of(p * piece, piece), n * piece)

    def rows_of(p, n):
        if n == 1:
            return rows_v[p]
        return jnp.concatenate([rows_v[p], rows_v[p + 1]], axis=1)

    live = lax.broadcasted_iota(jnp.int32, (block, piece), 0) < counts_ref[0, 0]
    own_rows = pl.ds(pl.multiple_of(shard * block, block), block)

    def mask_piece(p):
        values = grad_v[:, columns(p, 1)].astype(jnp.float32)
        rows_v[p, own_rows, :] = jnp.where(live, values, 0.0).astype(jnp.bfloat16)

    first_load.wait()
    mask_piece(0)
    mask_piece(1)
    pl.semaphore_wait(barrier, 7)

    def make_hidden(tile):
        rows = pl.ds(pl.multiple_of(tile * row_tile, row_tile), row_tile)
        gate_val, up_val, sig = activations(gate_v, up_v, rows)
        hidden_t[:, rows] = jnp.transpose(gate_val * sig * up_val).astype(jnp.bfloat16)

    def hidden_part(part):
        gate_load(part).wait()
        up_load(part).wait()
        for k in range(2):
            make_hidden(2 * part + k)

    def finish_rows(tile):
        rows = pl.ds(pl.multiple_of(tile * row_tile, row_tile), row_tile)
        gate_val, up_val, sig = activations(gate_v, up_v, rows)
        grad = d_hidden[rows, :]
        up_v[rows, :] = (grad * (gate_val * sig)).astype(jnp.bfloat16)
        slope = sig * (1.0 + gate_val * (1.0 - sig))
        gate_v[rows, :] = (grad * up_val * slope).astype(jnp.bfloat16)

    def stage_zero(u):
        def act(p, n):
            for target in (across_id, far_id, up_id, down_id):
                push(u, p, n, shard, target, 0)
            push(u, p, n, shard, sibling_id, 2)

        per_unit(u, act)

    def during(t, delay, body):
        @pl.when(jnp.logical_and(t >= delay, t < n_units + delay))
        def _():
            body(t - delay)

    def step(t, carry):
        def weight_grad(u):
            def act(p, n):
                arrived(u, n, 2, 8)
                grad = jnp.dot(hidden_t[...], rows_of(p, n), preferred_element_type=jnp.float32)
                total[:, columns(p, n)] = grad
                for k in range(n):
                    pair_out[p + k] = grad[:, k * piece : (k + 1) * piece].astype(jnp.bfloat16)
                    pair_copy(p + k).start()

            per_unit(u, act)

        def stage_two(u):
            def act(p, n):
                arrived(u, n, 1, 3)
                for step_y in (1, -1, 2):
                    push(u, p, n, at(z_other, step_y), sibling_id, 2)

            per_unit(u, act)

        def stage_one(u):
            def act(p, n):
                arrived(u, n, 0, 4)
                push(u, p, n, far_id, across_id, 1)
                push(u, p, n, across_id, up_id, 1)
                push(u, p, n, across_id, down_id, 1)
                for b in (across_id, up_id, down_id, far_id):
                    push(u, p, n, b, sibling_id, 2)

            per_unit(u, act)

        def data_grad(u):
            @pl.when(u >= 1)
            def _():
                p = 2 * u - 2
                weight_t[...] = jnp.transpose(master_v[:, columns(p, 2)]).astype(jnp.bfloat16)
                d_hidden[...] += jnp.dot(
                    rows_of(p, 2), weight_t[...], preferred_element_type=jnp.float32
                )

        def pair_sum(u):
            def act(p, n):
                for k in range(n):
                    pair_copy(p + k).wait_recv()
                    part = columns(p + k, 1)
                    both = total[:, part] + same_pair * pair_in[p + k].astype(jnp.float32)
                    total[:, part] = both
                    quad_out[p + k] = both.astype(jnp.bfloat16)
                    quad_copy(p + k).start()

            per_unit(u, act)

        def quad_sum(u):
            def act(p, n):
                for k in range(n):
                    quad_copy(p + k).wait_recv()
                    part = columns(p + k, 1)
                    whole = total[:, part] + same_quad * quad_in[p + k].astype(jnp.float32)
                    total[:, part] = whole
                    squares[...] += whole * whole

            per_unit(u, act)

        @pl.when(t < n_units - 1)
        def _():
            stage_zero(t + 1)

        during(t, 3, weight_grad)
        during(t, 1, stage_one)
        during(t, 2, stage_two)

        @pl.when(t == 0)
        def _():
            for part in range(2):
                hidden_part(part)
            rest_load.wait()

            @pl.loop(2, n_pieces)
            def _(p):
                mask_piece(p)

            squares[...] = jnp.zeros_like(squares)

        @pl.when(jnp.logical_and(t >= 1, t < 3))
        def _():
            hidden_part(t + 1)

        @pl.when(t == 3)
        def _():
            master_load.wait()
            d_hidden[...] = jnp.zeros_like(d_hidden)

        during(t, 3, data_grad)
        during(t, 4, pair_sum)

        @pl.when(jnp.logical_and(t >= n_units + 2, t < n_units + 4))
        def _():
            @pl.loop(0, n_tiles // 2)
            def _(k):
                finish_rows((t - n_units - 2) * (n_tiles // 2) + k)

        during(t, 6, quad_sum)
        return carry

    stage_zero(jnp.int32(0))
    lax.fori_loop(0, n_units + 6, step, 0)

    @pl.loop(0, n_units)
    def _(u):
        def act(p, n):
            blocks = some_blocks(n, 15)
            pltpu.make_async_copy(blocks, blocks, gather_send.at[u]).wait()
            for k in range(n):
                pair_copy(p + k).wait_send()
                quad_copy(p + k).wait_send()

        per_unit(u, act)


def finish(
    gate_v, up_v, master_v, total, squares, dgate_hbm, dup_hbm, new_hbm, new_v, store_sem
):
    n_rows, (n_hidden, width) = gate_v.shape[0], master_v.shape
    parts = 4
    copies = []
    for index, (src, dst) in enumerate(((gate_v, dgate_hbm), (up_v, dup_hbm))):
        for part in range(parts):
            rows = pl.ds(part * (n_rows // parts), n_rows // parts)
            copies.append(
                pltpu.make_async_copy(src.at[rows], dst.at[rows], store_sem.at[index, part])
            )

    def new_store(tile):
        rows = pl.ds(pl.multiple_of(tile * out_tile, out_tile), out_tile)
        return pltpu.make_async_copy(new_v.at[rows], new_hbm.at[rows], store_sem.at[2, tile])

    for copy in copies:
        copy.start()

    @pl.loop(0, n_hidden // out_tile)
    def _(tile):
        rows = pl.ds(pl.multiple_of(tile * out_tile, out_tile), out_tile)
        mean = jnp.sum(squares[rows, :], axis=1, keepdims=True) / width
        scale = learn_rate / jnp.sqrt(mean + rms_eps)
        new_v[rows, :] = master_v[rows, :] - total[rows, :] * scale
        new_store(tile).start()

    for copy in copies:
        copy.wait()

    @pl.loop(0, n_hidden // out_tile)
    def _(tile):
        new_store(tile).wait()


def per_device(grad_out, gate_pre, up_pre, counts, placement, master):
    block, width = grad_out.shape[1:]
    n_rows, n_hidden = gate_pre.shape[1:]
    n_pieces = width // piece
    n_units = n_pieces // 2 + 1
    hbm = pl.BlockSpec(memory_space=pl.ANY)
    smem = pl.BlockSpec(memory_space=pltpu.SMEM)
    vmem = pl.BlockSpec(memory_space=pltpu.VMEM)
    dma = pltpu.SemaphoreType.DMA
    pieces = (n_pieces, n_hidden, piece)
    held = pl.pallas_call(
        kernel,
        out_shape=(
            pltpu.VMEM((n_rows, n_hidden), jnp.bfloat16),
            pltpu.VMEM((n_rows, n_hidden), jnp.bfloat16),
            pltpu.VMEM((n_hidden, width), jnp.float32),
            pltpu.VMEM((n_hidden, width), jnp.float32),
            pltpu.VMEM((n_hidden, piece), jnp.float32),
        ),
        in_specs=[hbm, hbm, hbm, smem, smem, hbm],
        out_specs=(vmem,) * 5,
        scratch_shapes=[
            pltpu.VMEM((block, width), jnp.bfloat16),
            pltpu.VMEM((n_pieces, n_rows, piece), jnp.bfloat16),
            pltpu.VMEM((n_hidden, n_rows), jnp.bfloat16),
            pltpu.VMEM((n_rows, n_hidden), jnp.float32),
            pltpu.VMEM((chunk, n_hidden), jnp.bfloat16),
            pltpu.VMEM(pieces, jnp.bfloat16),
            pltpu.VMEM(pieces, jnp.bfloat16),
            pltpu.VMEM(pieces, jnp.bfloat16),
            pltpu.VMEM(pieces, jnp.bfloat16),
            dma((11,)),
            dma((n_units,)),
            dma((n_units, 3)),
            dma((n_pieces,)),
            dma((n_pieces,)),
            dma((n_pieces,)),
            dma((n_pieces,)),
        ],
        compiler_params=pltpu.CompilerParams(
            collective_id=0, has_side_effects=True, vmem_limit_bytes=40 * 2**20
        ),
    )(grad_out[0], gate_pre[0], up_pre[0], counts, placement, master[0])
    d_gate, d_up, new_master = pl.pallas_call(
        finish,
        out_shape=(
            jax.ShapeDtypeStruct((n_rows, n_hidden), jnp.bfloat16),
            jax.ShapeDtypeStruct((n_rows, n_hidden), jnp.bfloat16),
            jax.ShapeDtypeStruct((n_hidden, width), jnp.float32),
        ),
        in_specs=[vmem] * 5,
        out_specs=(hbm,) * 3,
        scratch_shapes=[pltpu.VMEM((n_hidden, width), jnp.float32), dma((3, 8))],
        compiler_params=pltpu.CompilerParams(vmem_limit_bytes=20 * 2**20),
    )(*held)
    return d_gate[None], d_up[None], new_master[None]


def solution(mesh):
    return jax.shard_map(
        per_device,
        mesh=mesh,
        in_specs=(
            P("expert", "shard", None),
            P("expert", None, "shard"),
            P("expert", None, "shard"),
            P("expert", "shard"),
            P(),
            P("expert", "shard", None),
        ),
        out_specs=(
            P("expert", None, "shard"),
            P("expert", None, "shard"),
            P("expert", "shard", None),
        ),
        check_vma=False,
    )
```

```python
import jax
import jax.numpy as jnp
from jax import lax
from jax.experimental import pallas as pl
from jax.experimental.pallas import tpu as pltpu
from jax.sharding import PartitionSpec as P

learn_rate = 0.02
rms_eps = 1e-06
piece = 128
chunk = 256
row_tile = 256
out_tile = 64
MESH = pl.DeviceIdType.MESH


def activations(gate_ref, up_ref, rows):
    gate_val = gate_ref[rows, :].astype(jnp.float32)
    up_val = up_ref[rows, :].astype(jnp.float32)
    return gate_val, up_val, lax.logistic(gate_val)


def kernel(
    grad_hbm, gate_hbm, up_hbm, counts_ref, place_ref, master_hbm,
    gate_v, up_v, master_v, total, squares,
    grad_v, rows_v, hidden_t, d_hidden, weight_t,
    pair_out, pair_in, quad_out, quad_in,
    load_sem, gather_send, gather_recv, pair_send, pair_recv, quad_send, quad_recv,
):
    expert, shard = lax.axis_index("expert"), lax.axis_index("shard")
    block, width = grad_v.shape
    n_pieces = width // piece
    n_units = n_pieces // 2 + 1
    n_rows, n_hidden = gate_v.shape
    n_tiles = n_rows // row_tile

    core = shard % 2
    y = (shard // 2) % 4
    z_base = (shard // 8) * 8
    z_other = (z_base + 8) % 16

    def at(base, step):
        return base + ((y + step + 4) % 4) * 2 + core

    up_id, down_id, far_id = at(z_base, 1), at(z_base, -1), at(z_base, 2)
    across_id = at(z_other, 0)
    sibling_id = shard + 1 - 2 * core
    way = 1 - 2 * core
    pair_id = expert + 1 - 2 * (expert % 2)
    quad_id = expert + 3 - 2 * (expert % 4)

    barrier = pltpu.get_barrier_semaphore()
    for peer in (
        (expert, up_id), (expert, down_id), (expert, far_id), (expert, across_id),
        (expert, at(z_other, 1)), (expert, at(z_other, -1)), (expert, at(z_other, 2)),
        (expert, sibling_id), (pair_id, shard), (quad_id, shard),
    ):
        pl.semaphore_signal(barrier, inc=1, device_id=peer, device_id_type=MESH)

    def load(src, dst, index):
        return pltpu.make_async_copy(src, dst, load_sem.at[index])

    quarter = n_rows // 4

    def gate_load(part):
        rows = pl.ds(pl.multiple_of(part * quarter, quarter), quarter)
        return load(gate_hbm.at[rows], gate_v.at[rows], 3 + part)

    def up_load(part):
        rows = pl.ds(pl.multiple_of(part * quarter, quarter), quarter)
        return load(up_hbm.at[rows], up_v.at[rows], 7 + part)

    first, rest = pl.ds(0, chunk), pl.ds(chunk, width - chunk)
    first_load = load(grad_hbm.at[:, first], grad_v.at[:, first], 0)
    rest_load = load(grad_hbm.at[:, rest], grad_v.at[:, rest], 1)
    master_load = load(master_hbm, master_v, 2)
    first_load.start()
    for part in range(4):
        gate_load(part).start()
        up_load(part).start()
    rest_load.start()
    master_load.start()

    same_pair = jnp.where(place_ref[expert] == place_ref[pair_id], 1.0, 0.0)
    same_quad = jnp.where(place_ref[expert] == place_ref[quad_id], 1.0, 0.0)

    def block_of(p, n, b):
        return rows_v.at[pl.ds(p, n), pl.ds(pl.multiple_of(b * block, block), block)]

    def some_blocks(n, k):
        return rows_v.at[pl.ds(0, n), pl.ds(0, k * block)]

    def per_unit(u, act):
        @pl.when(u < 2)
        def _():
            act(u, 1)

        @pl.when(u >= 2)
        def _():
            act(2 * u - 2, 2)

    def push(u, p, n, b, target, stage):
        pltpu.make_async_remote_copy(
            src_ref=block_of(p, n, b),
            dst_ref=block_of(p, n, b),
            send_sem=gather_send.at[u],
            recv_sem=gather_recv.at[u, stage],
            device_id=(expert, target),
            device_id_type=MESH,
        ).start()

    def arrived(u, n, stage, k):
        blocks = some_blocks(n, k)
        pltpu.make_async_copy(blocks, blocks, gather_recv.at[u, stage]).wait()

    quarter_rows = n_hidden // 4

    def part_rows(q):
        return pl.ds(0, n_hidden) if q is None else pl.ds(q * quarter_rows, quarter_rows)

    def exchange(out, landing, send_sem, recv_sem, target, p, q):
        index = p if q is None else p + q
        return pltpu.make_async_remote_copy(
            src_ref=out.at[p, part_rows(q)],
            dst_ref=landing.at[p, part_rows(q)],
            send_sem=send_sem.at[index],
            recv_sem=recv_sem.at[index],
            device_id=(target, shard),
            device_id_type=MESH,
        )

    def pair_copy(p, q):
        return exchange(pair_out, pair_in, pair_send, pair_recv, pair_id, p, q)

    def quad_copy(p, q):
        return exchange(quad_out, quad_in, quad_send, quad_recv, quad_id, p, q)

    def per_part(u, p, n, act):
        act(p, None)
        if n == 2:
            @pl.when(u < n_units - 1)
            def _():
                act(p + 1, None)

            @pl.when(u == n_units - 1)
            def _():
                for q in range(4):
                    act(n_pieces - 1, q)

    def columns(p, n):
        return pl.ds(pl.multiple_of(p * piece, piece), n * piece)

    def rows_of(p, n):
        if n == 1:
            return rows_v[p]
        return jnp.concatenate([rows_v[p], rows_v[p + 1]], axis=1)

    live = lax.broadcasted_iota(jnp.int32, (block, piece), 0) < counts_ref[0, 0]
    own_rows = pl.ds(pl.multiple_of(shard * block, block), block)

    def mask_piece(p):
        values = grad_v[:, columns(p, 1)].astype(jnp.float32)
        rows_v[p, own_rows, :] = jnp.where(live, values, 0.0).astype(jnp.bfloat16)

    first_load.wait()
    mask_piece(0)
    mask_piece(1)
    pl.semaphore_wait(barrier, 10)

    def make_hidden(tile):
        rows = pl.ds(pl.multiple_of(tile * row_tile, row_tile), row_tile)
        gate_val, up_val, sig = activations(gate_v, up_v, rows)
        hidden_t[:, rows] = jnp.transpose(gate_val * sig * up_val).astype(jnp.bfloat16)

    def hidden_part(part):
        gate_load(part).wait()
        up_load(part).wait()
        for k in range(2):
            make_hidden(2 * part + k)

    def finish_rows(tile):
        rows = pl.ds(pl.multiple_of(tile * row_tile, row_tile), row_tile)
        gate_val, up_val, sig = activations(gate_v, up_v, rows)
        grad = d_hidden[rows, :]
        up_v[rows, :] = (grad * (gate_val * sig)).astype(jnp.bfloat16)
        slope = sig * (1.0 + gate_val * (1.0 - sig))
        gate_v[rows, :] = (grad * up_val * slope).astype(jnp.bfloat16)

    def stage_zero(u):
        def act(p, n):
            targets = (across_id, far_id, up_id, down_id)
            if n == 1:
                targets = (at(z_other, 2), at(z_other, 1), at(z_other, -1)) + targets
            for target in targets:
                push(u, p, n, shard, target, 0)
            push(u, p, n, shard, sibling_id, 2)

        per_unit(u, act)

    def during(t, delay, body):
        @pl.when(jnp.logical_and(t >= delay, t < n_units + delay))
        def _():
            body(t - delay)

    def step(t, carry):
        def weight_grad(u):
            def act(p, n):
                arrived(u, n, 2, 8)
                grad = jnp.dot(hidden_t[...], rows_of(p, n), preferred_element_type=jnp.float32)
                total[:, columns(p, n)] = grad
                for k in range(n):
                    pair_out[p + k] = grad[:, k * piece : (k + 1) * piece].astype(jnp.bfloat16)
                per_part(u, p, n, lambda p, q: pair_copy(p, q).start())

            return act

        def stage_two(u):
            @pl.when(u >= 2)
            def _():
                arrived(u, 2, 1, 3)
                for step_y in (1, -1, 2):
                    push(u, 2 * u - 2, 2, at(z_other, step_y), sibling_id, 2)

        def stage_one(u):
            def act(p, n):
                blocks = (across_id, up_id, down_id, far_id)
                if n == 1:
                    arrived(u, n, 0, 7)
                    blocks += (at(z_other, 1), at(z_other, -1), at(z_other, 2))
                else:
                    arrived(u, n, 0, 4)
                    push(u, p, n, far_id, across_id, 1)
                    push(u, p, n, across_id, up_id, 1)
                    push(u, p, n, across_id, down_id, 1)
                for b in blocks:
                    push(u, p, n, b, sibling_id, 2)

            per_unit(u, act)

        def data_grad(u):
            @pl.when(u >= 1)
            def _():
                p = 2 * u - 2
                weight_t[...] = jnp.transpose(master_v[:, columns(p, 2)]).astype(jnp.bfloat16)
                d_hidden[...] += jnp.dot(
                    rows_of(p, 2), weight_t[...], preferred_element_type=jnp.float32
                )

        def pair_sum(u):
            def one(p, q):
                pair_copy(p, q).wait_recv()
                rows, cols = part_rows(q), columns(p, 1)
                received = pair_in[p, rows, :].astype(jnp.float32)
                both = total[rows, cols] + same_pair * received
                total[rows, cols] = both
                quad_out[p, rows, :] = both.astype(jnp.bfloat16)
                quad_copy(p, q).start()

            per_unit(u, lambda p, n: per_part(u, p, n, one))

        def quad_sum(u):
            def one(p, q):
                quad_copy(p, q).wait_recv()
                rows, cols = part_rows(q), columns(p, 1)
                received = quad_in[p, rows, :].astype(jnp.float32)
                whole = total[rows, cols] + same_quad * received
                total[rows, cols] = whole
                squares[rows, :] += whole * whole

            per_unit(u, lambda p, n: per_part(u, p, n, one))

        @pl.when(jnp.logical_and(t >= 2, t < 4))
        def _():
            weight_grad(t - 2)(t - 2, 1)

        @pl.when(jnp.logical_and(t >= 5, t < n_units + 3))
        def _():
            weight_grad(t - 3)(2 * (t - 3) - 2, 2)

        during(t, 1, stage_one)
        during(t, 2, stage_two)

        @pl.when(t < n_units - 1)
        def _():
            stage_zero(t + 1)

        @pl.when(t == 0)
        def _():
            for part in range(2):
                hidden_part(part)
            rest_load.wait()

            @pl.loop(2, n_pieces)
            def _(p):
                mask_piece(p)

            squares[...] = jnp.zeros_like(squares)

        @pl.when(t == 1)
        def _():
            for part in range(2, 4):
                hidden_part(part)

        @pl.when(t == 3)
        def _():
            master_load.wait()
            d_hidden[...] = jnp.zeros_like(d_hidden)

        during(t, 3, data_grad)
        during(t, 4, pair_sum)

        @pl.when(jnp.logical_and(t >= n_units + 2, t < n_units + 4))
        def _():
            @pl.loop(0, n_tiles // 2)
            def _(k):
                finish_rows((t - n_units - 2) * (n_tiles // 2) + k)

        during(t, 6, quad_sum)
        return carry

    stage_zero(jnp.int32(0))
    lax.fori_loop(0, n_units + 6, step, 0)

    @pl.loop(0, n_units)
    def _(u):
        def act(p, n):
            blocks = some_blocks(n, 15)
            pltpu.make_async_copy(blocks, blocks, gather_send.at[u]).wait()

            def sent(p, q):
                pair_copy(p, q).wait_send()
                quad_copy(p, q).wait_send()

            per_part(u, p, n, sent)

        per_unit(u, act)


def finish(
    gate_v, up_v, master_v, total, squares, dgate_hbm, dup_hbm, new_hbm, new_v, store_sem
):
    n_rows, (n_hidden, width) = gate_v.shape[0], master_v.shape
    parts = 4
    copies = []
    for index, (src, dst) in enumerate(((gate_v, dgate_hbm), (up_v, dup_hbm))):
        for part in range(parts):
            rows = pl.ds(part * (n_rows // parts), n_rows // parts)
            copies.append(
                pltpu.make_async_copy(src.at[rows], dst.at[rows], store_sem.at[index, part])
            )

    def new_store(tile):
        rows = pl.ds(pl.multiple_of(tile * out_tile, out_tile), out_tile)
        return pltpu.make_async_copy(new_v.at[rows], new_hbm.at[rows], store_sem.at[2, tile])

    for copy in copies:
        copy.start()

    @pl.loop(0, n_hidden // out_tile)
    def _(tile):
        rows = pl.ds(pl.multiple_of(tile * out_tile, out_tile), out_tile)
        mean = jnp.sum(squares[rows, :], axis=1, keepdims=True) / width
        scale = learn_rate / jnp.sqrt(mean + rms_eps)
        new_v[rows, :] = master_v[rows, :] - total[rows, :] * scale
        new_store(tile).start()

    for copy in copies:
        copy.wait()

    @pl.loop(0, n_hidden // out_tile)
    def _(tile):
        new_store(tile).wait()


def per_device(grad_out, gate_pre, up_pre, counts, placement, master):
    block, width = grad_out.shape[1:]
    n_rows, n_hidden = gate_pre.shape[1:]
    n_pieces = width // piece
    n_units = n_pieces // 2 + 1
    hbm = pl.BlockSpec(memory_space=pl.ANY)
    smem = pl.BlockSpec(memory_space=pltpu.SMEM)
    vmem = pl.BlockSpec(memory_space=pltpu.VMEM)
    dma = pltpu.SemaphoreType.DMA
    pieces = (n_pieces, n_hidden, piece)
    held = pl.pallas_call(
        kernel,
        out_shape=(
            pltpu.VMEM((n_rows, n_hidden), jnp.bfloat16),
            pltpu.VMEM((n_rows, n_hidden), jnp.bfloat16),
            pltpu.VMEM((n_hidden, width), jnp.float32),
            pltpu.VMEM((n_hidden, width), jnp.float32),
            pltpu.VMEM((n_hidden, piece), jnp.float32),
        ),
        in_specs=[hbm, hbm, hbm, smem, smem, hbm],
        out_specs=(vmem,) * 5,
        scratch_shapes=[
            pltpu.VMEM((block, width), jnp.bfloat16),
            pltpu.VMEM((n_pieces, n_rows, piece), jnp.bfloat16),
            pltpu.VMEM((n_hidden, n_rows), jnp.bfloat16),
            pltpu.VMEM((n_rows, n_hidden), jnp.float32),
            pltpu.VMEM((chunk, n_hidden), jnp.bfloat16),
            pltpu.VMEM(pieces, jnp.bfloat16),
            pltpu.VMEM(pieces, jnp.bfloat16),
            pltpu.VMEM(pieces, jnp.bfloat16),
            pltpu.VMEM(pieces, jnp.bfloat16),
            dma((11,)),
            dma((n_units,)),
            dma((n_units, 3)),
            dma((n_pieces + 3,)),
            dma((n_pieces + 3,)),
            dma((n_pieces + 3,)),
            dma((n_pieces + 3,)),
        ],
        compiler_params=pltpu.CompilerParams(
            collective_id=0, has_side_effects=True, vmem_limit_bytes=40 * 2**20
        ),
    )(grad_out[0], gate_pre[0], up_pre[0], counts, placement, master[0])
    d_gate, d_up, new_master = pl.pallas_call(
        finish,
        out_shape=(
            jax.ShapeDtypeStruct((n_rows, n_hidden), jnp.bfloat16),
            jax.ShapeDtypeStruct((n_rows, n_hidden), jnp.bfloat16),
            jax.ShapeDtypeStruct((n_hidden, width), jnp.float32),
        ),
        in_specs=[vmem] * 5,
        out_specs=(hbm,) * 3,
        scratch_shapes=[pltpu.VMEM((n_hidden, width), jnp.float32), dma((3, 8))],
        compiler_params=pltpu.CompilerParams(vmem_limit_bytes=20 * 2**20),
    )(*held)
    return d_gate[None], d_up[None], new_master[None]


def solution(mesh):
    return jax.shard_map(
        per_device,
        mesh=mesh,
        in_specs=(
            P("expert", "shard", None),
            P("expert", None, "shard"),
            P("expert", None, "shard"),
            P("expert", "shard"),
            P(),
            P("expert", "shard", None),
        ),
        out_specs=(
            P("expert", None, "shard"),
            P("expert", None, "shard"),
            P("expert", "shard", None),
        ),
        check_vma=False,
    )
```

```python
import jax
import jax.numpy as jnp
from jax import lax
from jax.experimental import pallas as pl
from jax.experimental.pallas import tpu as pltpu
from jax.sharding import PartitionSpec as P

learn_rate = 0.02
rms_eps = 1e-06
piece = 128
chunk = 256
row_tile = 256
out_tile = 64
MESH = pl.DeviceIdType.MESH


def activations(gate_ref, up_ref, rows):
    gate_val = gate_ref[rows, :].astype(jnp.float32)
    up_val = up_ref[rows, :].astype(jnp.float32)
    return gate_val, up_val, lax.logistic(gate_val)


def kernel(
    grad_hbm, gate_hbm, up_hbm, counts_ref, place_ref, master_hbm,
    gate_v, up_v, master_v, total, squares,
    grad_v, rows_v, hidden_t, d_hidden, weight_t,
    first_out, first_in, second_out, second_in,
    load_sem, gather_send, gather_recv, first_send, first_recv, second_send, second_recv,
):
    expert, shard = lax.axis_index("expert"), lax.axis_index("shard")
    block, width = grad_v.shape
    n_pieces = width // piece
    n_units = n_pieces // 2 + 1
    n_rows, n_hidden = gate_v.shape
    n_tiles = n_rows // row_tile

    core = shard % 2
    y = (shard // 2) % 4
    z_base = (shard // 8) * 8
    z_other = (z_base + 8) % 16

    def at(base, step):
        return base + ((y + step + 4) % 4) * 2 + core

    up_id, down_id, far_id = at(z_base, 1), at(z_base, -1), at(z_base, 2)
    across_id = at(z_other, 0)
    sibling_id = shard + 1 - 2 * core
    way = 1 - 2 * core
    pair_id = expert + 1 - 2 * (expert % 2)
    quad_id = expert + 3 - 2 * (expert % 4)

    barrier = pltpu.get_barrier_semaphore()
    for peer in (
        (expert, up_id), (expert, down_id), (expert, far_id), (expert, across_id),
        (expert, sibling_id), (pair_id, shard), (quad_id, shard),
    ):
        pl.semaphore_signal(barrier, inc=1, device_id=peer, device_id_type=MESH)

    def load(src, dst, index):
        return pltpu.make_async_copy(src, dst, load_sem.at[index])

    quarter = n_rows // 4

    def gate_load(part):
        rows = pl.ds(pl.multiple_of(part * quarter, quarter), quarter)
        return load(gate_hbm.at[rows], gate_v.at[rows], 3 + part)

    def up_load(part):
        rows = pl.ds(pl.multiple_of(part * quarter, quarter), quarter)
        return load(up_hbm.at[rows], up_v.at[rows], 7 + part)

    first, rest = pl.ds(0, chunk), pl.ds(chunk, width - chunk)
    first_load = load(grad_hbm.at[:, first], grad_v.at[:, first], 0)
    rest_load = load(grad_hbm.at[:, rest], grad_v.at[:, rest], 1)
    master_load = load(master_hbm, master_v, 2)
    first_load.start()
    for part in range(4):
        gate_load(part).start()
        up_load(part).start()
    rest_load.start()
    master_load.start()

    same_pair = jnp.where(place_ref[expert] == place_ref[pair_id], 1.0, 0.0)
    same_quad = jnp.where(place_ref[expert] == place_ref[quad_id], 1.0, 0.0)

    def block_of(p, n, b):
        return rows_v.at[pl.ds(p, n), pl.ds(pl.multiple_of(b * block, block), block)]

    def some_blocks(n, k):
        return rows_v.at[pl.ds(0, n), pl.ds(0, k * block)]

    def per_unit(u, act):
        @pl.when(u < 2)
        def _():
            act(u, 1)

        @pl.when(u >= 2)
        def _():
            act(2 * u - 2, 2)

    def push(u, p, n, b, target, stage):
        pltpu.make_async_remote_copy(
            src_ref=block_of(p, n, b),
            dst_ref=block_of(p, n, b),
            send_sem=gather_send.at[u],
            recv_sem=gather_recv.at[u, stage],
            device_id=(expert, target),
            device_id_type=MESH,
        ).start()

    def arrived(u, n, stage, k):
        blocks = some_blocks(n, k)
        pltpu.make_async_copy(blocks, blocks, gather_recv.at[u, stage]).wait()

    quarter_rows = n_hidden // 4

    def part_rows(q):
        return pl.ds(0, n_hidden) if q is None else pl.ds(q * quarter_rows, quarter_rows)

    def exchange(out, landing, send_sem, recv_sem, swap, p, q):
        index = p if q is None else n_pieces - 2 + 4 * (p - n_pieces + 2) + q
        odd = (p + swap) % 2
        return pltpu.make_async_remote_copy(
            src_ref=out.at[p, part_rows(q)],
            dst_ref=landing.at[p, part_rows(q)],
            send_sem=send_sem.at[index],
            recv_sem=recv_sem.at[index],
            device_id=(pair_id * (1 - odd) + quad_id * odd, shard),
            device_id_type=MESH,
        )

    def first_copy(p, q):
        return exchange(first_out, first_in, first_send, first_recv, 0, p, q)

    def second_copy(p, q):
        return exchange(second_out, second_in, second_send, second_recv, 1, p, q)

    def same_expert(p, swap):
        odd = jnp.asarray((p + swap) % 2, jnp.float32)
        return same_pair * (1.0 - odd) + same_quad * odd

    def per_part(u, p, n, act):
        if n == 1:
            act(p, None)
        else:
            @pl.when(u < n_units - 1)
            def _():
                act(p, None)
                act(p + 1, None)

            @pl.when(u == n_units - 1)
            def _():
                for q in range(4):
                    act(n_pieces - 2, q)
                    act(n_pieces - 1, q)

    def columns(p, n):
        return pl.ds(pl.multiple_of(p * piece, piece), n * piece)

    def rows_of(p, n):
        if n == 1:
            return rows_v[p]
        return jnp.concatenate([rows_v[p], rows_v[p + 1]], axis=1)

    live = lax.broadcasted_iota(jnp.int32, (block, piece), 0) < counts_ref[0, 0]
    own_rows = pl.ds(pl.multiple_of(shard * block, block), block)

    def mask_piece(p):
        values = grad_v[:, columns(p, 1)].astype(jnp.float32)
        rows_v[p, own_rows, :] = jnp.where(live, values, 0.0).astype(jnp.bfloat16)

    first_load.wait()
    mask_piece(0)
    mask_piece(1)
    pl.semaphore_wait(barrier, 7)

    def make_hidden(tile):
        rows = pl.ds(pl.multiple_of(tile * row_tile, row_tile), row_tile)
        gate_val, up_val, sig = activations(gate_v, up_v, rows)
        hidden_t[:, rows] = jnp.transpose(gate_val * sig * up_val).astype(jnp.bfloat16)

    def hidden_part(part):
        gate_load(part).wait()
        up_load(part).wait()
        for k in range(2):
            make_hidden(2 * part + k)

    def finish_rows(tile):
        rows = pl.ds(pl.multiple_of(tile * row_tile, row_tile), row_tile)
        gate_val, up_val, sig = activations(gate_v, up_v, rows)
        grad = d_hidden[rows, :]
        up_v[rows, :] = (grad * (gate_val * sig)).astype(jnp.bfloat16)
        slope = sig * (1.0 + gate_val * (1.0 - sig))
        gate_v[rows, :] = (grad * up_val * slope).astype(jnp.bfloat16)

    def stage_zero(u):
        def act(p, n):
            for target in (across_id, far_id, up_id, down_id):
                push(u, p, n, shard, target, 0)
            push(u, p, n, shard, sibling_id, 2)

        per_unit(u, act)

    def during(t, delay, body):
        @pl.when(jnp.logical_and(t >= delay, t < n_units + delay))
        def _():
            body(t - delay)

    def step(t, carry):
        def weight_grad(u):
            def act(p, n):
                arrived(u, n, 2, 8)
                grad = jnp.dot(hidden_t[...], rows_of(p, n), preferred_element_type=jnp.float32)
                total[:, columns(p, n)] = grad
                for k in range(n):
                    first_out[p + k] = grad[:, k * piece : (k + 1) * piece].astype(jnp.bfloat16)
                per_part(u, p, n, lambda p, q: first_copy(p, q).start())

            per_unit(u, act)

        def stage_two(u):
            def act(p, n):
                arrived(u, n, 1, 3)
                for step_y in (1, -1, 2):
                    push(u, p, n, at(z_other, step_y), sibling_id, 2)

            per_unit(u, act)

        def stage_one(u):
            def act(p, n):
                arrived(u, n, 0, 4)
                push(u, p, n, far_id, across_id, 1)
                push(u, p, n, across_id, up_id, 1)
                push(u, p, n, across_id, down_id, 1)
                for b in (across_id, up_id, down_id, far_id):
                    push(u, p, n, b, sibling_id, 2)

            per_unit(u, act)

        def data_grad(u):
            @pl.when(u >= 1)
            def _():
                p = 2 * u - 2
                weight_t[...] = jnp.transpose(master_v[:, columns(p, 2)]).astype(jnp.bfloat16)
                d_hidden[...] += jnp.dot(
                    rows_of(p, 2), weight_t[...], preferred_element_type=jnp.float32
                )

        def first_sum(u):
            def one(p, q):
                first_copy(p, q).wait_recv()
                rows, cols = part_rows(q), columns(p, 1)
                received = first_in[p, rows, :].astype(jnp.float32)
                both = total[rows, cols] + same_expert(p, 0) * received
                total[rows, cols] = both
                second_out[p, rows, :] = both.astype(jnp.bfloat16)
                second_copy(p, q).start()

            per_unit(u, lambda p, n: per_part(u, p, n, one))

        def second_sum(u):
            def one(p, q):
                second_copy(p, q).wait_recv()
                rows, cols = part_rows(q), columns(p, 1)
                received = second_in[p, rows, :].astype(jnp.float32)
                whole = total[rows, cols] + same_expert(p, 1) * received
                total[rows, cols] = whole
                squares[rows, :] += whole * whole

            per_unit(u, lambda p, n: per_part(u, p, n, one))

        during(t, 3, weight_grad)
        during(t, 1, stage_one)
        during(t, 2, stage_two)

        @pl.when(t < n_units - 1)
        def _():
            stage_zero(t + 1)

        @pl.when(t == 0)
        def _():
            for part in range(2):
                hidden_part(part)
            rest_load.wait()

            @pl.loop(2, n_pieces)
            def _(p):
                mask_piece(p)

            squares[...] = jnp.zeros_like(squares)

        @pl.when(t == 1)
        def _():
            for part in range(2, 4):
                hidden_part(part)

        @pl.when(t == 3)
        def _():
            master_load.wait()
            d_hidden[...] = jnp.zeros_like(d_hidden)

        during(t, 3, data_grad)
        during(t, 4, first_sum)

        @pl.when(jnp.logical_and(t >= n_units + 2, t < n_units + 4))
        def _():
            @pl.loop(0, n_tiles // 2)
            def _(k):
                finish_rows((t - n_units - 2) * (n_tiles // 2) + k)

        during(t, 6, second_sum)
        return carry

    stage_zero(jnp.int32(0))
    lax.fori_loop(0, n_units + 6, step, 0)

    @pl.loop(0, n_units)
    def _(u):
        def act(p, n):
            blocks = some_blocks(n, 15)
            pltpu.make_async_copy(blocks, blocks, gather_send.at[u]).wait()

            def sent(p, q):
                first_copy(p, q).wait_send()
                second_copy(p, q).wait_send()

            per_part(u, p, n, sent)

        per_unit(u, act)


def finish(
    gate_v, up_v, master_v, total, squares, dgate_hbm, dup_hbm, new_hbm, new_v, store_sem
):
    n_rows, (n_hidden, width) = gate_v.shape[0], master_v.shape
    parts = 4
    copies = []
    for index, (src, dst) in enumerate(((gate_v, dgate_hbm), (up_v, dup_hbm))):
        for part in range(parts):
            rows = pl.ds(part * (n_rows // parts), n_rows // parts)
            copies.append(
                pltpu.make_async_copy(src.at[rows], dst.at[rows], store_sem.at[index, part])
            )

    def new_store(tile):
        rows = pl.ds(pl.multiple_of(tile * out_tile, out_tile), out_tile)
        return pltpu.make_async_copy(new_v.at[rows], new_hbm.at[rows], store_sem.at[2, tile])

    for copy in copies:
        copy.start()

    @pl.loop(0, n_hidden // out_tile)
    def _(tile):
        rows = pl.ds(pl.multiple_of(tile * out_tile, out_tile), out_tile)
        mean = jnp.sum(squares[rows, :], axis=1, keepdims=True) / width
        scale = learn_rate / jnp.sqrt(mean + rms_eps)
        new_v[rows, :] = master_v[rows, :] - total[rows, :] * scale
        new_store(tile).start()

    for copy in copies:
        copy.wait()

    @pl.loop(0, n_hidden // out_tile)
    def _(tile):
        new_store(tile).wait()


def per_device(grad_out, gate_pre, up_pre, counts, placement, master):
    block, width = grad_out.shape[1:]
    n_rows, n_hidden = gate_pre.shape[1:]
    n_pieces = width // piece
    n_units = n_pieces // 2 + 1
    hbm = pl.BlockSpec(memory_space=pl.ANY)
    smem = pl.BlockSpec(memory_space=pltpu.SMEM)
    vmem = pl.BlockSpec(memory_space=pltpu.VMEM)
    dma = pltpu.SemaphoreType.DMA
    pieces = (n_pieces, n_hidden, piece)
    held = pl.pallas_call(
        kernel,
        out_shape=(
            pltpu.VMEM((n_rows, n_hidden), jnp.bfloat16),
            pltpu.VMEM((n_rows, n_hidden), jnp.bfloat16),
            pltpu.VMEM((n_hidden, width), jnp.float32),
            pltpu.VMEM((n_hidden, width), jnp.float32),
            pltpu.VMEM((n_hidden, piece), jnp.float32),
        ),
        in_specs=[hbm, hbm, hbm, smem, smem, hbm],
        out_specs=(vmem,) * 5,
        scratch_shapes=[
            pltpu.VMEM((block, width), jnp.bfloat16),
            pltpu.VMEM((n_pieces, n_rows, piece), jnp.bfloat16),
            pltpu.VMEM((n_hidden, n_rows), jnp.bfloat16),
            pltpu.VMEM((n_rows, n_hidden), jnp.float32),
            pltpu.VMEM((chunk, n_hidden), jnp.bfloat16),
            pltpu.VMEM(pieces, jnp.bfloat16),
            pltpu.VMEM(pieces, jnp.bfloat16),
            pltpu.VMEM(pieces, jnp.bfloat16),
            pltpu.VMEM(pieces, jnp.bfloat16),
            dma((11,)),
            dma((n_units,)),
            dma((n_units, 3)),
            dma((n_pieces + 6,)),
            dma((n_pieces + 6,)),
            dma((n_pieces + 6,)),
            dma((n_pieces + 6,)),
        ],
        compiler_params=pltpu.CompilerParams(
            collective_id=0, has_side_effects=True, vmem_limit_bytes=40 * 2**20
        ),
    )(grad_out[0], gate_pre[0], up_pre[0], counts, placement, master[0])
    d_gate, d_up, new_master = pl.pallas_call(
        finish,
        out_shape=(
            jax.ShapeDtypeStruct((n_rows, n_hidden), jnp.bfloat16),
            jax.ShapeDtypeStruct((n_rows, n_hidden), jnp.bfloat16),
            jax.ShapeDtypeStruct((n_hidden, width), jnp.float32),
        ),
        in_specs=[vmem] * 5,
        out_specs=(hbm,) * 3,
        scratch_shapes=[pltpu.VMEM((n_hidden, width), jnp.float32), dma((3, 8))],
        compiler_params=pltpu.CompilerParams(vmem_limit_bytes=20 * 2**20),
    )(*held)
    return d_gate[None], d_up[None], new_master[None]


def solution(mesh):
    return jax.shard_map(
        per_device,
        mesh=mesh,
        in_specs=(
            P("expert", "shard", None),
            P("expert", None, "shard"),
            P("expert", None, "shard"),
            P("expert", "shard"),
            P(),
            P("expert", "shard", None),
        ),
        out_specs=(
            P("expert", None, "shard"),
            P("expert", None, "shard"),
            P("expert", "shard", None),
        ),
        check_vma=False,
    )
```

```python
import jax
import jax.numpy as jnp
from jax import lax
from jax.experimental import pallas as pl
from jax.experimental.pallas import tpu as pltpu
from jax.sharding import PartitionSpec as P

learn_rate = 0.02
rms_eps = 1e-06
piece = 128
chunk = 256
row_tile = 256
out_tile = 64
MESH = pl.DeviceIdType.MESH


def activations(gate_ref, up_ref, rows):
    gate_val = gate_ref[rows, :].astype(jnp.float32)
    up_val = up_ref[rows, :].astype(jnp.float32)
    return gate_val, up_val, lax.logistic(gate_val)


def kernel(
    grad_hbm, gate_hbm, up_hbm, counts_ref, place_ref, master_hbm,
    gate_v, up_v, master_v, total, squares,
    grad_v, rows_v, hidden_t, d_hidden, weight_t,
    first_out, first_in, second_out, second_in,
    load_sem, gather_send, gather_recv, first_send, first_recv, second_send, second_recv,
):
    expert, shard = lax.axis_index("expert"), lax.axis_index("shard")
    block, width = grad_v.shape
    n_pieces = width // piece
    n_units = n_pieces // 2
    n_rows, n_hidden = gate_v.shape
    n_tiles = n_rows // row_tile

    core = shard % 2
    y = (shard // 2) % 4
    z_base = (shard // 8) * 8
    z_other = (z_base + 8) % 16

    def at(base, step):
        return base + ((y + step + 4) % 4) * 2 + core

    up_id, down_id, far_id = at(z_base, 1), at(z_base, -1), at(z_base, 2)
    across_id = at(z_other, 0)
    sibling_id = shard + 1 - 2 * core
    way = 1 - 2 * core
    pair_id = expert + 1 - 2 * (expert % 2)
    quad_id = expert + 3 - 2 * (expert % 4)

    barrier = pltpu.get_barrier_semaphore()
    for peer in (
        (expert, up_id), (expert, down_id), (expert, far_id), (expert, across_id),
        (expert, sibling_id), (pair_id, shard), (quad_id, shard),
    ):
        pl.semaphore_signal(barrier, inc=1, device_id=peer, device_id_type=MESH)

    def load(src, dst, index):
        return pltpu.make_async_copy(src, dst, load_sem.at[index])

    quarter = n_rows // 4

    def gate_load(part):
        rows = pl.ds(pl.multiple_of(part * quarter, quarter), quarter)
        return load(gate_hbm.at[rows], gate_v.at[rows], 3 + part)

    def up_load(part):
        rows = pl.ds(pl.multiple_of(part * quarter, quarter), quarter)
        return load(up_hbm.at[rows], up_v.at[rows], 7 + part)

    first, rest = pl.ds(0, chunk), pl.ds(chunk, width - chunk)
    first_load = load(grad_hbm.at[:, first], grad_v.at[:, first], 0)
    rest_load = load(grad_hbm.at[:, rest], grad_v.at[:, rest], 1)
    master_load = load(master_hbm, master_v, 2)
    first_load.start()
    for part in range(4):
        gate_load(part).start()
        up_load(part).start()
    rest_load.start()
    master_load.start()

    same_pair = jnp.where(place_ref[expert] == place_ref[pair_id], 1.0, 0.0)
    same_quad = jnp.where(place_ref[expert] == place_ref[quad_id], 1.0, 0.0)

    def block_of(p, n, b):
        return rows_v.at[pl.ds(p, n), pl.ds(pl.multiple_of(b * block, block), block)]

    def some_blocks(n, k):
        return rows_v.at[pl.ds(0, n), pl.ds(0, k * block)]

    def per_unit(u, act):
        act(2 * u, 2)

    def push(u, p, n, b, target, stage):
        pltpu.make_async_remote_copy(
            src_ref=block_of(p, n, b),
            dst_ref=block_of(p, n, b),
            send_sem=gather_send.at[u],
            recv_sem=gather_recv.at[u, stage],
            device_id=(expert, target),
            device_id_type=MESH,
        ).start()

    def arrived(u, n, stage, k):
        blocks = some_blocks(n, k)
        pltpu.make_async_copy(blocks, blocks, gather_recv.at[u, stage]).wait()

    quarter_rows = n_hidden // 4

    def part_rows(q):
        return pl.ds(0, n_hidden) if q is None else pl.ds(q * quarter_rows, quarter_rows)

    def exchange(out, landing, send_sem, recv_sem, swap, p, q):
        index = p if q is None else n_pieces - 2 + 4 * (p - n_pieces + 2) + q
        odd = (p + swap) % 2
        return pltpu.make_async_remote_copy(
            src_ref=out.at[p, part_rows(q)],
            dst_ref=landing.at[p, part_rows(q)],
            send_sem=send_sem.at[index],
            recv_sem=recv_sem.at[index],
            device_id=(pair_id * (1 - odd) + quad_id * odd, shard),
            device_id_type=MESH,
        )

    def first_copy(p, q):
        return exchange(first_out, first_in, first_send, first_recv, 0, p, q)

    def second_copy(p, q):
        return exchange(second_out, second_in, second_send, second_recv, 1, p, q)

    def same_expert(p, swap):
        odd = jnp.asarray((p + swap) % 2, jnp.float32)
        return same_pair * (1.0 - odd) + same_quad * odd

    def per_part(u, p, n, act):
        if n == 1:
            act(p, None)
        else:
            @pl.when(u < n_units - 1)
            def _():
                act(p, None)
                act(p + 1, None)

            @pl.when(u == n_units - 1)
            def _():
                for q in range(4):
                    act(n_pieces - 2, q)
                    act(n_pieces - 1, q)

    def columns(p, n):
        return pl.ds(pl.multiple_of(p * piece, piece), n * piece)

    def rows_of(p, n):
        if n == 1:
            return rows_v[p]
        return jnp.concatenate([rows_v[p], rows_v[p + 1]], axis=1)

    live = lax.broadcasted_iota(jnp.int32, (block, piece), 0) < counts_ref[0, 0]
    own_rows = pl.ds(pl.multiple_of(shard * block, block), block)

    def mask_piece(p):
        values = grad_v[:, columns(p, 1)].astype(jnp.float32)
        rows_v[p, own_rows, :] = jnp.where(live, values, 0.0).astype(jnp.bfloat16)

    first_load.wait()
    mask_piece(0)
    mask_piece(1)
    pl.semaphore_wait(barrier, 7)

    def make_hidden(tile):
        rows = pl.ds(pl.multiple_of(tile * row_tile, row_tile), row_tile)
        gate_val, up_val, sig = activations(gate_v, up_v, rows)
        hidden_t[:, rows] = jnp.transpose(gate_val * sig * up_val).astype(jnp.bfloat16)

    def hidden_part(part):
        gate_load(part).wait()
        up_load(part).wait()
        for k in range(2):
            make_hidden(2 * part + k)

    def finish_rows(tile):
        rows = pl.ds(pl.multiple_of(tile * row_tile, row_tile), row_tile)
        gate_val, up_val, sig = activations(gate_v, up_v, rows)
        grad = d_hidden[rows, :]
        up_v[rows, :] = (grad * (gate_val * sig)).astype(jnp.bfloat16)
        slope = sig * (1.0 + gate_val * (1.0 - sig))
        gate_v[rows, :] = (grad * up_val * slope).astype(jnp.bfloat16)

    def stage_zero(u):
        def act(p, n):
            for target in (across_id, far_id, up_id, down_id):
                push(u, p, n, shard, target, 0)
            push(u, p, n, shard, sibling_id, 2)

        per_unit(u, act)

    def during(t, delay, body):
        @pl.when(jnp.logical_and(t >= delay, t < n_units + delay))
        def _():
            body(t - delay)

    def step(t, carry):
        def weight_grad(u):
            def act(p, n):
                arrived(u, n, 2, 8)
                grad = jnp.dot(hidden_t[...], rows_of(p, n), preferred_element_type=jnp.float32)
                total[:, columns(p, n)] = grad
                for k in range(n):
                    first_out[p + k] = grad[:, k * piece : (k + 1) * piece].astype(jnp.bfloat16)
                per_part(u, p, n, lambda p, q: first_copy(p, q).start())

            per_unit(u, act)

        def stage_two(u):
            def act(p, n):
                arrived(u, n, 1, 3)
                for step_y in (1, -1, 2):
                    push(u, p, n, at(z_other, step_y), sibling_id, 2)

            per_unit(u, act)

        def stage_one(u):
            def act(p, n):
                arrived(u, n, 0, 4)
                push(u, p, n, far_id, across_id, 1)
                push(u, p, n, across_id, up_id, 1)
                push(u, p, n, across_id, down_id, 1)
                for b in (across_id, up_id, down_id, far_id):
                    push(u, p, n, b, sibling_id, 2)

            per_unit(u, act)

        def data_grad(u):
            def add(p):
                weight_t[...] = jnp.transpose(master_v[:, columns(p, 2)]).astype(jnp.bfloat16)
                d_hidden[...] += jnp.dot(
                    rows_of(p, 2), weight_t[...], preferred_element_type=jnp.float32
                )

            add(2 * u)

        def first_sum(u):
            def one(p, q):
                first_copy(p, q).wait_recv()
                rows, cols = part_rows(q), columns(p, 1)
                received = first_in[p, rows, :].astype(jnp.float32)
                both = total[rows, cols] + same_expert(p, 0) * received
                total[rows, cols] = both
                second_out[p, rows, :] = both.astype(jnp.bfloat16)
                second_copy(p, q).start()

            per_unit(u, lambda p, n: per_part(u, p, n, one))

        def second_sum(u):
            def one(p, q):
                second_copy(p, q).wait_recv()
                rows, cols = part_rows(q), columns(p, 1)
                received = second_in[p, rows, :].astype(jnp.float32)
                whole = total[rows, cols] + same_expert(p, 1) * received
                total[rows, cols] = whole
                squares[rows, :] += whole * whole
                first_copy(p, q).wait_send()
                second_copy(p, q).wait_send()

            def act(p, n):
                blocks = some_blocks(n, 15)
                pltpu.make_async_copy(blocks, blocks, gather_send.at[u]).wait()
                per_part(u, p, n, one)

            per_unit(u, act)

        during(t, 3, weight_grad)
        during(t, 1, stage_one)
        during(t, 2, stage_two)

        @pl.when(t == 0)
        def _():
            hidden_part(0)
            rest_load.wait()

            @pl.loop(2, n_pieces)
            def _(p):
                mask_piece(p)

            squares[...] = jnp.zeros_like(squares)

        @pl.when(t < n_units - 1)
        def _():
            stage_zero(t + 1)

        @pl.when(t == 1)
        def _():
            hidden_part(1)

        @pl.when(t == 2)
        def _():
            for part in range(2, 4):
                hidden_part(part)

        @pl.when(t == 3)
        def _():
            master_load.wait()
            d_hidden[...] = jnp.zeros_like(d_hidden)

        during(t, 3, data_grad)
        during(t, 4, first_sum)

        @pl.when(jnp.logical_and(t >= n_units + 2, t < n_units + 4))
        def _():
            @pl.loop(0, n_tiles // 2)
            def _(k):
                finish_rows((t - n_units - 2) * (n_tiles // 2) + k)

        during(t, 6, second_sum)
        return carry

    stage_zero(jnp.int32(0))
    lax.fori_loop(0, n_units + 6, step, 0)


def finish(
    gate_v, up_v, master_v, total, squares, dgate_hbm, dup_hbm, new_hbm, new_v, store_sem
):
    n_rows, (n_hidden, width) = gate_v.shape[0], master_v.shape
    parts = 4
    copies = []
    for index, (src, dst) in enumerate(((gate_v, dgate_hbm), (up_v, dup_hbm))):
        for part in range(parts):
            rows = pl.ds(part * (n_rows // parts), n_rows // parts)
            copies.append(
                pltpu.make_async_copy(src.at[rows], dst.at[rows], store_sem.at[index, part])
            )

    def new_store(tile):
        rows = pl.ds(pl.multiple_of(tile * out_tile, out_tile), out_tile)
        return pltpu.make_async_copy(new_v.at[rows], new_hbm.at[rows], store_sem.at[2, tile])

    for copy in copies:
        copy.start()

    @pl.loop(0, n_hidden // out_tile)
    def _(tile):
        rows = pl.ds(pl.multiple_of(tile * out_tile, out_tile), out_tile)
        mean = jnp.sum(squares[rows, :], axis=1, keepdims=True) / width
        scale = learn_rate / jnp.sqrt(mean + rms_eps)
        new_v[rows, :] = master_v[rows, :] - total[rows, :] * scale
        new_store(tile).start()

    for copy in copies:
        copy.wait()

    @pl.loop(0, n_hidden // out_tile)
    def _(tile):
        new_store(tile).wait()


def per_device(grad_out, gate_pre, up_pre, counts, placement, master):
    block, width = grad_out.shape[1:]
    n_rows, n_hidden = gate_pre.shape[1:]
    n_pieces = width // piece
    n_units = n_pieces // 2
    hbm = pl.BlockSpec(memory_space=pl.ANY)
    smem = pl.BlockSpec(memory_space=pltpu.SMEM)
    vmem = pl.BlockSpec(memory_space=pltpu.VMEM)
    dma = pltpu.SemaphoreType.DMA
    pieces = (n_pieces, n_hidden, piece)
    held = pl.pallas_call(
        kernel,
        out_shape=(
            pltpu.VMEM((n_rows, n_hidden), jnp.bfloat16),
            pltpu.VMEM((n_rows, n_hidden), jnp.bfloat16),
            pltpu.VMEM((n_hidden, width), jnp.float32),
            pltpu.VMEM((n_hidden, width), jnp.float32),
            pltpu.VMEM((n_hidden, piece), jnp.float32),
        ),
        in_specs=[hbm, hbm, hbm, smem, smem, hbm],
        out_specs=(vmem,) * 5,
        scratch_shapes=[
            pltpu.VMEM((block, width), jnp.bfloat16),
            pltpu.VMEM((n_pieces, n_rows, piece), jnp.bfloat16),
            pltpu.VMEM((n_hidden, n_rows), jnp.bfloat16),
            pltpu.VMEM((n_rows, n_hidden), jnp.float32),
            pltpu.VMEM((chunk, n_hidden), jnp.bfloat16),
            pltpu.VMEM(pieces, jnp.bfloat16),
            pltpu.VMEM(pieces, jnp.bfloat16),
            pltpu.VMEM(pieces, jnp.bfloat16),
            pltpu.VMEM(pieces, jnp.bfloat16),
            dma((11,)),
            dma((n_units,)),
            dma((n_units, 3)),
            dma((n_pieces + 6,)),
            dma((n_pieces + 6,)),
            dma((n_pieces + 6,)),
            dma((n_pieces + 6,)),
        ],
        compiler_params=pltpu.CompilerParams(
            collective_id=0, has_side_effects=True, vmem_limit_bytes=40 * 2**20
        ),
    )(grad_out[0], gate_pre[0], up_pre[0], counts, placement, master[0])
    d_gate, d_up, new_master = pl.pallas_call(
        finish,
        out_shape=(
            jax.ShapeDtypeStruct((n_rows, n_hidden), jnp.bfloat16),
            jax.ShapeDtypeStruct((n_rows, n_hidden), jnp.bfloat16),
            jax.ShapeDtypeStruct((n_hidden, width), jnp.float32),
        ),
        in_specs=[vmem] * 5,
        out_specs=(hbm,) * 3,
        scratch_shapes=[pltpu.VMEM((n_hidden, width), jnp.float32), dma((3, 8))],
        compiler_params=pltpu.CompilerParams(vmem_limit_bytes=20 * 2**20),
    )(*held)
    return d_gate[None], d_up[None], new_master[None]


def solution(mesh):
    return jax.shard_map(
        per_device,
        mesh=mesh,
        in_specs=(
            P("expert", "shard", None),
            P("expert", None, "shard"),
            P("expert", None, "shard"),
            P("expert", "shard"),
            P(),
            P("expert", "shard", None),
        ),
        out_specs=(
            P("expert", None, "shard"),
            P("expert", None, "shard"),
            P("expert", "shard", None),
        ),
        check_vma=False,
    )
```

```python
import jax
import jax.numpy as jnp
from jax import lax
from jax.experimental import pallas as pl
from jax.experimental.pallas import tpu as pltpu
from jax.sharding import PartitionSpec as P

learn_rate = 0.02
rms_eps = 1e-06
piece = 128
chunk = 256
row_tile = 256
out_tile = 64
MESH = pl.DeviceIdType.MESH


def activations(gate_ref, up_ref, rows):
    gate_val = gate_ref[rows, :].astype(jnp.float32)
    up_val = up_ref[rows, :].astype(jnp.float32)
    return gate_val, up_val, lax.logistic(gate_val)


def kernel(
    grad_hbm, gate_hbm, up_hbm, counts_ref, place_ref, master_hbm,
    gate_v, up_v, master_v, total, squares,
    grad_v, rows_v, hidden_t, d_hidden, weight_t,
    first_out, first_in, second_out, second_in,
    load_sem, gather_send, gather_recv, first_send, first_recv, second_send, second_recv,
):
    expert, shard = lax.axis_index("expert"), lax.axis_index("shard")
    block, width = grad_v.shape
    n_pieces = width // piece
    n_units = n_pieces // 2
    n_rows, n_hidden = gate_v.shape
    n_tiles = n_rows // row_tile

    core = shard % 2
    y = (shard // 2) % 4
    z_base = (shard // 8) * 8
    z_other = (z_base + 8) % 16

    def at(base, step):
        return base + ((y + step + 4) % 4) * 2 + core

    up_id, down_id, far_id = at(z_base, 1), at(z_base, -1), at(z_base, 2)
    across_id = at(z_other, 0)
    sibling_id = shard + 1 - 2 * core
    way = 1 - 2 * core
    pair_id = expert + 1 - 2 * (expert % 2)
    quad_id = expert + 3 - 2 * (expert % 4)

    def load(src, dst, index):
        return pltpu.make_async_copy(src, dst, load_sem.at[index])

    quarter = n_rows // 4

    def gate_load(part):
        rows = pl.ds(pl.multiple_of(part * quarter, quarter), quarter)
        return load(gate_hbm.at[rows], gate_v.at[rows], 3 + part)

    def up_load(part):
        rows = pl.ds(pl.multiple_of(part * quarter, quarter), quarter)
        return load(up_hbm.at[rows], up_v.at[rows], 7 + part)

    first, rest = pl.ds(0, chunk), pl.ds(chunk, width - chunk)
    first_load = load(grad_hbm.at[:, first], grad_v.at[:, first], 0)
    rest_load = load(grad_hbm.at[:, rest], grad_v.at[:, rest], 1)
    master_load = load(master_hbm, master_v, 2)
    first_load.start()
    rest_load.start()

    barrier = pltpu.get_barrier_semaphore()
    for peer in (
        (expert, up_id), (expert, down_id), (expert, far_id), (expert, across_id),
        (expert, sibling_id), (pair_id, shard), (quad_id, shard),
    ):
        pl.semaphore_signal(barrier, inc=1, device_id=peer, device_id_type=MESH)

    for part in range(4):
        gate_load(part).start()
        up_load(part).start()
    master_load.start()

    same_pair = jnp.where(place_ref[expert] == place_ref[pair_id], 1.0, 0.0)
    same_quad = jnp.where(place_ref[expert] == place_ref[quad_id], 1.0, 0.0)

    def block_of(p, n, b):
        return rows_v.at[pl.ds(p, n), pl.ds(pl.multiple_of(b * block, block), block)]

    def some_blocks(n, k):
        return rows_v.at[pl.ds(0, n), pl.ds(0, k * block)]

    def per_unit(u, act):
        act(2 * u, 2)

    def push(u, p, n, b, target, stage):
        pltpu.make_async_remote_copy(
            src_ref=block_of(p, n, b),
            dst_ref=block_of(p, n, b),
            send_sem=gather_send.at[u],
            recv_sem=gather_recv.at[u, stage],
            device_id=(expert, target),
            device_id_type=MESH,
        ).start()

    def arrived(u, n, stage, k):
        blocks = some_blocks(n, k)
        pltpu.make_async_copy(blocks, blocks, gather_recv.at[u, stage]).wait()

    quarter_rows = n_hidden // 4

    def part_rows(q):
        return pl.ds(0, n_hidden) if q is None else pl.ds(q * quarter_rows, quarter_rows)

    def exchange(out, landing, send_sem, recv_sem, swap, p, q):
        index = p if q is None else n_pieces - 2 + 4 * (p - n_pieces + 2) + q
        odd = (p + swap) % 2
        return pltpu.make_async_remote_copy(
            src_ref=out.at[p, part_rows(q)],
            dst_ref=landing.at[p, part_rows(q)],
            send_sem=send_sem.at[index],
            recv_sem=recv_sem.at[index],
            device_id=(pair_id * (1 - odd) + quad_id * odd, shard),
            device_id_type=MESH,
        )

    def first_copy(p, q):
        return exchange(first_out, first_in, first_send, first_recv, 0, p, q)

    def second_copy(p, q):
        return exchange(second_out, second_in, second_send, second_recv, 1, p, q)

    def same_expert(p, swap):
        odd = jnp.asarray((p + swap) % 2, jnp.float32)
        return same_pair * (1.0 - odd) + same_quad * odd

    def per_part(u, p, n, act):
        if n == 1:
            act(p, None)
        else:
            @pl.when(u < n_units - 1)
            def _():
                act(p, None)
                act(p + 1, None)

            @pl.when(u == n_units - 1)
            def _():
                for q in range(4):
                    act(n_pieces - 2, q)
                    act(n_pieces - 1, q)

    def columns(p, n):
        return pl.ds(pl.multiple_of(p * piece, piece), n * piece)

    def rows_of(p, n):
        if n == 1:
            return rows_v[p]
        return jnp.concatenate([rows_v[p], rows_v[p + 1]], axis=1)

    live = lax.broadcasted_iota(jnp.int32, (block, piece), 0) < counts_ref[0, 0]
    own_rows = pl.ds(pl.multiple_of(shard * block, block), block)

    def mask_piece(p):
        values = grad_v[:, columns(p, 1)].astype(jnp.float32)
        rows_v[p, own_rows, :] = jnp.where(live, values, 0.0).astype(jnp.bfloat16)

    first_load.wait()
    mask_piece(0)
    mask_piece(1)
    pl.semaphore_wait(barrier, 7)

    def make_hidden(tile):
        rows = pl.ds(pl.multiple_of(tile * row_tile, row_tile), row_tile)
        gate_val, up_val, sig = activations(gate_v, up_v, rows)
        hidden_t[:, rows] = jnp.transpose(gate_val * sig * up_val).astype(jnp.bfloat16)

    def hidden_part(part):
        gate_load(part).wait()
        up_load(part).wait()
        for k in range(2):
            make_hidden(2 * part + k)

    def finish_rows(tile):
        rows = pl.ds(pl.multiple_of(tile * row_tile, row_tile), row_tile)
        gate_val, up_val, sig = activations(gate_v, up_v, rows)
        grad = d_hidden[rows, :]
        up_v[rows, :] = (grad * (gate_val * sig)).astype(jnp.bfloat16)
        slope = sig * (1.0 + gate_val * (1.0 - sig))
        gate_v[rows, :] = (grad * up_val * slope).astype(jnp.bfloat16)

    def stage_zero(u):
        def act(p, n):
            for target in (across_id, far_id, up_id, down_id):
                push(u, p, n, shard, target, 0)
            push(u, p, n, shard, sibling_id, 2)

        per_unit(u, act)

    def during(t, delay, body):
        @pl.when(jnp.logical_and(t >= delay, t < n_units + delay))
        def _():
            body(t - delay)

    def step(t, carry):
        def weight_grad(u):
            def act(p, n):
                arrived(u, n, 2, 8)
                grad = jnp.dot(hidden_t[...], rows_of(p, n), preferred_element_type=jnp.float32)
                total[:, columns(p, n)] = grad
                for k in range(n):
                    first_out[p + k] = grad[:, k * piece : (k + 1) * piece].astype(jnp.bfloat16)
                per_part(u, p, n, lambda p, q: first_copy(p, q).start())

            per_unit(u, act)

        def stage_two(u):
            def act(p, n):
                arrived(u, n, 1, 3)
                for step_y in (1, -1, 2):
                    push(u, p, n, at(z_other, step_y), sibling_id, 2)

            per_unit(u, act)

        def stage_one(u):
            def act(p, n):
                arrived(u, n, 0, 4)
                push(u, p, n, far_id, across_id, 1)
                push(u, p, n, across_id, up_id, 1)
                push(u, p, n, across_id, down_id, 1)
                for b in (across_id, up_id, down_id, far_id):
                    push(u, p, n, b, sibling_id, 2)

            per_unit(u, act)

        def data_grad(u):
            def add(p):
                weight_t[...] = jnp.transpose(master_v[:, columns(p, 2)]).astype(jnp.bfloat16)
                d_hidden[...] += jnp.dot(
                    rows_of(p, 2), weight_t[...], preferred_element_type=jnp.float32
                )

            add(2 * u)

        def first_sum(u):
            def one(p, q):
                first_copy(p, q).wait_recv()
                rows, cols = part_rows(q), columns(p, 1)
                received = first_in[p, rows, :].astype(jnp.float32)
                both = total[rows, cols] + same_expert(p, 0) * received
                total[rows, cols] = both
                second_out[p, rows, :] = both.astype(jnp.bfloat16)
                second_copy(p, q).start()

            per_unit(u, lambda p, n: per_part(u, p, n, one))

        def second_sum(u):
            def one(p, q):
                second_copy(p, q).wait_recv()
                rows, cols = part_rows(q), columns(p, 1)
                received = second_in[p, rows, :].astype(jnp.float32)
                whole = total[rows, cols] + same_expert(p, 1) * received
                total[rows, cols] = whole
                squares[rows, :] += whole * whole
                first_copy(p, q).wait_send()
                second_copy(p, q).wait_send()

            def act(p, n):
                blocks = some_blocks(n, 15)
                pltpu.make_async_copy(blocks, blocks, gather_send.at[u]).wait()
                per_part(u, p, n, one)

            per_unit(u, act)

        during(t, 3, weight_grad)
        during(t, 1, stage_one)
        during(t, 2, stage_two)

        @pl.when(t == 0)
        def _():
            rest_load.wait()

            mask_piece(2)
            mask_piece(3)

        @pl.when(t == 1)
        def _():
            @pl.loop(4, n_pieces)
            def _(p):
                mask_piece(p)

            squares[...] = jnp.zeros_like(squares)

        @pl.when(t < n_units - 1)
        def _():
            stage_zero(t + 1)

        @pl.when(t < 2)
        def _():
            hidden_part(t)

        @pl.when(t == 2)
        def _():
            for part in range(2, 4):
                hidden_part(part)

        @pl.when(t == 3)
        def _():
            master_load.wait()
            d_hidden[...] = jnp.zeros_like(d_hidden)

        during(t, 3, data_grad)
        during(t, 4, first_sum)

        @pl.when(jnp.logical_and(t >= n_units + 2, t < n_units + 4))
        def _():
            @pl.loop(0, n_tiles // 2)
            def _(k):
                finish_rows((t - n_units - 2) * (n_tiles // 2) + k)

        during(t, 6, second_sum)
        return carry

    stage_zero(jnp.int32(0))
    lax.fori_loop(0, n_units + 6, step, 0)


def finish(
    gate_v, up_v, master_v, total, squares, dgate_hbm, dup_hbm, new_hbm, new_v, store_sem
):
    n_rows, (n_hidden, width) = gate_v.shape[0], master_v.shape
    parts = 4
    copies = []
    for index, (src, dst) in enumerate(((gate_v, dgate_hbm), (up_v, dup_hbm))):
        for part in range(parts):
            rows = pl.ds(part * (n_rows // parts), n_rows // parts)
            copies.append(
                pltpu.make_async_copy(src.at[rows], dst.at[rows], store_sem.at[index, part])
            )

    def new_store(tile):
        rows = pl.ds(pl.multiple_of(tile * out_tile, out_tile), out_tile)
        return pltpu.make_async_copy(new_v.at[rows], new_hbm.at[rows], store_sem.at[2, tile])

    for copy in copies:
        copy.start()

    @pl.loop(0, n_hidden // out_tile)
    def _(tile):
        rows = pl.ds(pl.multiple_of(tile * out_tile, out_tile), out_tile)
        mean = jnp.sum(squares[rows, :], axis=1, keepdims=True) / width
        scale = learn_rate / jnp.sqrt(mean + rms_eps)
        new_v[rows, :] = master_v[rows, :] - total[rows, :] * scale
        new_store(tile).start()

    for copy in copies:
        copy.wait()

    @pl.loop(0, n_hidden // out_tile)
    def _(tile):
        new_store(tile).wait()


def per_device(grad_out, gate_pre, up_pre, counts, placement, master):
    block, width = grad_out.shape[1:]
    n_rows, n_hidden = gate_pre.shape[1:]
    n_pieces = width // piece
    n_units = n_pieces // 2
    hbm = pl.BlockSpec(memory_space=pl.ANY)
    smem = pl.BlockSpec(memory_space=pltpu.SMEM)
    vmem = pl.BlockSpec(memory_space=pltpu.VMEM)
    dma = pltpu.SemaphoreType.DMA
    pieces = (n_pieces, n_hidden, piece)
    held = pl.pallas_call(
        kernel,
        out_shape=(
            pltpu.VMEM((n_rows, n_hidden), jnp.bfloat16),
            pltpu.VMEM((n_rows, n_hidden), jnp.bfloat16),
            pltpu.VMEM((n_hidden, width), jnp.float32),
            pltpu.VMEM((n_hidden, width), jnp.float32),
            pltpu.VMEM((n_hidden, piece), jnp.float32),
        ),
        in_specs=[hbm, hbm, hbm, smem, smem, hbm],
        out_specs=(vmem,) * 5,
        scratch_shapes=[
            pltpu.VMEM((block, width), jnp.bfloat16),
            pltpu.VMEM((n_pieces, n_rows, piece), jnp.bfloat16),
            pltpu.VMEM((n_hidden, n_rows), jnp.bfloat16),
            pltpu.VMEM((n_rows, n_hidden), jnp.float32),
            pltpu.VMEM((chunk, n_hidden), jnp.bfloat16),
            pltpu.VMEM(pieces, jnp.bfloat16),
            pltpu.VMEM(pieces, jnp.bfloat16),
            pltpu.VMEM(pieces, jnp.bfloat16),
            pltpu.VMEM(pieces, jnp.bfloat16),
            dma((11,)),
            dma((n_units,)),
            dma((n_units, 3)),
            dma((n_pieces + 6,)),
            dma((n_pieces + 6,)),
            dma((n_pieces + 6,)),
            dma((n_pieces + 6,)),
        ],
        compiler_params=pltpu.CompilerParams(
            collective_id=0, has_side_effects=True, vmem_limit_bytes=40 * 2**20
        ),
    )(grad_out[0], gate_pre[0], up_pre[0], counts, placement, master[0])
    d_gate, d_up, new_master = pl.pallas_call(
        finish,
        out_shape=(
            jax.ShapeDtypeStruct((n_rows, n_hidden), jnp.bfloat16),
            jax.ShapeDtypeStruct((n_rows, n_hidden), jnp.bfloat16),
            jax.ShapeDtypeStruct((n_hidden, width), jnp.float32),
        ),
        in_specs=[vmem] * 5,
        out_specs=(hbm,) * 3,
        scratch_shapes=[pltpu.VMEM((n_hidden, width), jnp.float32), dma((3, 8))],
        compiler_params=pltpu.CompilerParams(vmem_limit_bytes=20 * 2**20),
    )(*held)
    return d_gate[None], d_up[None], new_master[None]


def solution(mesh):
    return jax.shard_map(
        per_device,
        mesh=mesh,
        in_specs=(
            P("expert", "shard", None),
            P("expert", None, "shard"),
            P("expert", None, "shard"),
            P("expert", "shard"),
            P(),
            P("expert", "shard", None),
        ),
        out_specs=(
            P("expert", None, "shard"),
            P("expert", None, "shard"),
            P("expert", "shard", None),
        ),
        check_vma=False,
    )
```

```python
import jax
import jax.numpy as jnp
from jax import lax
from jax.experimental import pallas as pl
from jax.experimental.pallas import tpu as pltpu
from jax.sharding import PartitionSpec as P

learn_rate = 0.02
rms_eps = 1e-06
piece = 128
chunk = 256
row_tile = 256
out_tile = 128
last_parts = 8
MESH = pl.DeviceIdType.MESH


def activations(gate_ref, up_ref, rows):
    gate_val = gate_ref[rows, :].astype(jnp.float32)
    up_val = up_ref[rows, :].astype(jnp.float32)
    return gate_val, up_val, lax.logistic(gate_val)


def kernel(
    grad_hbm, gate_hbm, up_hbm, counts_ref, place_ref, master_hbm,
    gate_v, up_v, master_v, total, squares,
    grad_v, rows_v, hidden_t, d_hidden, weight_t,
    first_out, first_in, second_out, second_in,
    load_sem, gather_send, gather_recv, first_send, first_recv, second_send, second_recv,
):
    expert, shard = lax.axis_index("expert"), lax.axis_index("shard")
    block, width = grad_v.shape
    n_pieces = width // piece
    n_units = n_pieces // 2
    n_rows, n_hidden = gate_v.shape
    n_tiles = n_rows // row_tile

    core = shard % 2
    y = (shard // 2) % 4
    z_base = (shard // 8) * 8
    z_other = (z_base + 8) % 16

    def at(base, step):
        return base + ((y + step + 4) % 4) * 2 + core

    up_id, down_id, far_id = at(z_base, 1), at(z_base, -1), at(z_base, 2)
    across_id = at(z_other, 0)
    sibling_id = shard + 1 - 2 * core
    way = 1 - 2 * core
    pair_id = expert + 1 - 2 * (expert % 2)
    quad_id = expert + 3 - 2 * (expert % 4)

    def load(src, dst, index):
        return pltpu.make_async_copy(src, dst, load_sem.at[index])

    quarter = n_rows // 4

    def gate_load(part):
        rows = pl.ds(pl.multiple_of(part * quarter, quarter), quarter)
        return load(gate_hbm.at[rows], gate_v.at[rows], 3 + part)

    def up_load(part):
        rows = pl.ds(pl.multiple_of(part * quarter, quarter), quarter)
        return load(up_hbm.at[rows], up_v.at[rows], 7 + part)

    first, rest = pl.ds(0, chunk), pl.ds(chunk, width - chunk)
    first_load = load(grad_hbm.at[:, first], grad_v.at[:, first], 0)
    rest_load = load(grad_hbm.at[:, rest], grad_v.at[:, rest], 1)
    master_load = load(master_hbm, master_v, 2)
    first_load.start()
    rest_load.start()

    barrier = pltpu.get_barrier_semaphore()
    for peer in (
        (expert, up_id), (expert, down_id), (expert, far_id), (expert, across_id),
        (expert, sibling_id), (pair_id, shard), (quad_id, shard),
    ):
        pl.semaphore_signal(barrier, inc=1, device_id=peer, device_id_type=MESH)

    for part in range(4):
        gate_load(part).start()
        up_load(part).start()
    master_load.start()

    same_pair = jnp.where(place_ref[expert] == place_ref[pair_id], 1.0, 0.0)
    same_quad = jnp.where(place_ref[expert] == place_ref[quad_id], 1.0, 0.0)

    def block_of(p, n, b):
        return rows_v.at[pl.ds(p, n), pl.ds(pl.multiple_of(b * block, block), block)]

    def some_blocks(n, k):
        return rows_v.at[pl.ds(0, n), pl.ds(0, k * block)]

    def per_unit(u, act):
        act(2 * u, 2)

    def push(u, p, n, b, target, stage):
        pltpu.make_async_remote_copy(
            src_ref=block_of(p, n, b),
            dst_ref=block_of(p, n, b),
            send_sem=gather_send.at[u],
            recv_sem=gather_recv.at[u, stage],
            device_id=(expert, target),
            device_id_type=MESH,
        ).start()

    def arrived(u, n, stage, k):
        blocks = some_blocks(n, k)
        pltpu.make_async_copy(blocks, blocks, gather_recv.at[u, stage]).wait()

    quarter_rows = n_hidden // last_parts

    def part_rows(q):
        return pl.ds(0, n_hidden) if q is None else pl.ds(q * quarter_rows, quarter_rows)

    def exchange(out, landing, send_sem, recv_sem, swap, p, q):
        index = p if q is None else n_pieces - 2 + last_parts * (p - n_pieces + 2) + q
        odd = (p + swap) % 2
        return pltpu.make_async_remote_copy(
            src_ref=out.at[p, part_rows(q)],
            dst_ref=landing.at[p, part_rows(q)],
            send_sem=send_sem.at[index],
            recv_sem=recv_sem.at[index],
            device_id=(pair_id * (1 - odd) + quad_id * odd, shard),
            device_id_type=MESH,
        )

    def first_copy(p, q):
        return exchange(first_out, first_in, first_send, first_recv, 0, p, q)

    def second_copy(p, q):
        return exchange(second_out, second_in, second_send, second_recv, 1, p, q)

    def same_expert(p, swap):
        odd = jnp.asarray((p + swap) % 2, jnp.float32)
        return same_pair * (1.0 - odd) + same_quad * odd

    def per_part(u, p, n, act):
        if n == 1:
            act(p, None)
        else:
            @pl.when(u < n_units - 1)
            def _():
                act(p, None)
                act(p + 1, None)

            @pl.when(u == n_units - 1)
            def _():
                for q in range(last_parts):
                    act(n_pieces - 2, q)
                    act(n_pieces - 1, q)

    def columns(p, n):
        return pl.ds(pl.multiple_of(p * piece, piece), n * piece)

    def rows_of(p, n):
        if n == 1:
            return rows_v[p]
        return jnp.concatenate([rows_v[p], rows_v[p + 1]], axis=1)

    live = lax.broadcasted_iota(jnp.int32, (block, piece), 0) < counts_ref[0, 0]
    own_rows = pl.ds(pl.multiple_of(shard * block, block), block)

    def mask_piece(p):
        values = grad_v[:, columns(p, 1)].astype(jnp.float32)
        rows_v[p, own_rows, :] = jnp.where(live, values, 0.0).astype(jnp.bfloat16)

    first_load.wait()
    mask_piece(0)
    mask_piece(1)
    pl.semaphore_wait(barrier, 7)

    def make_hidden(tile):
        rows = pl.ds(pl.multiple_of(tile * row_tile, row_tile), row_tile)
        gate_val, up_val, sig = activations(gate_v, up_v, rows)
        hidden_t[:, rows] = jnp.transpose(gate_val * sig * up_val).astype(jnp.bfloat16)

    def hidden_part(part):
        gate_load(part).wait()
        up_load(part).wait()
        for k in range(2):
            make_hidden(2 * part + k)

    def finish_rows(tile):
        rows = pl.ds(pl.multiple_of(tile * row_tile, row_tile), row_tile)
        gate_val, up_val, sig = activations(gate_v, up_v, rows)
        grad = d_hidden[rows, :]
        up_v[rows, :] = (grad * (gate_val * sig)).astype(jnp.bfloat16)
        slope = sig * (1.0 + gate_val * (1.0 - sig))
        gate_v[rows, :] = (grad * up_val * slope).astype(jnp.bfloat16)

    def stage_zero(u):
        def act(p, n):
            for target in (across_id, far_id, up_id, down_id):
                push(u, p, n, shard, target, 0)
            push(u, p, n, shard, sibling_id, 2)

        per_unit(u, act)

    def during(t, delay, body):
        @pl.when(jnp.logical_and(t >= delay, t < n_units + delay))
        def _():
            body(t - delay)

    def step(t, carry):
        def weight_grad(u):
            def act(p, n):
                arrived(u, n, 2, 8)
                grad = jnp.dot(hidden_t[...], rows_of(p, n), preferred_element_type=jnp.float32)
                total[:, columns(p, n)] = grad
                for k in range(n):
                    first_out[p + k] = grad[:, k * piece : (k + 1) * piece].astype(jnp.bfloat16)
                per_part(u, p, n, lambda p, q: first_copy(p, q).start())

            per_unit(u, act)

        def stage_two(u):
            def act(p, n):
                arrived(u, n, 1, 3)
                for step_y in (1, -1, 2):
                    push(u, p, n, at(z_other, step_y), sibling_id, 2)

            per_unit(u, act)

        def stage_one(u):
            def act(p, n):
                arrived(u, n, 0, 4)
                push(u, p, n, far_id, across_id, 1)
                push(u, p, n, across_id, up_id, 1)
                push(u, p, n, across_id, down_id, 1)
                for b in (across_id, up_id, down_id, far_id):
                    push(u, p, n, b, sibling_id, 2)

            per_unit(u, act)

        def data_grad(u):
            def add(p):
                weight_t[...] = jnp.transpose(master_v[:, columns(p, 2)]).astype(jnp.bfloat16)
                d_hidden[...] += jnp.dot(
                    rows_of(p, 2), weight_t[...], preferred_element_type=jnp.float32
                )

            add(2 * u)

        def first_sum(u):
            def one(p, q):
                first_copy(p, q).wait_recv()
                rows, cols = part_rows(q), columns(p, 1)
                received = first_in[p, rows, :].astype(jnp.float32)
                both = total[rows, cols] + same_expert(p, 0) * received
                total[rows, cols] = both
                second_out[p, rows, :] = both.astype(jnp.bfloat16)
                second_copy(p, q).start()

            per_unit(u, lambda p, n: per_part(u, p, n, one))

        def second_sum(u):
            def one(p, q):
                second_copy(p, q).wait_recv()
                rows, cols = part_rows(q), columns(p, 1)
                received = second_in[p, rows, :].astype(jnp.float32)
                whole = total[rows, cols] + same_expert(p, 1) * received
                total[rows, cols] = whole
                squares[rows, :] += whole * whole
                first_copy(p, q).wait_send()
                second_copy(p, q).wait_send()

            def act(p, n):
                blocks = some_blocks(n, 15)
                pltpu.make_async_copy(blocks, blocks, gather_send.at[u]).wait()
                per_part(u, p, n, one)

            per_unit(u, act)

        during(t, 3, weight_grad)
        during(t, 1, stage_one)
        during(t, 2, stage_two)

        @pl.when(t == 0)
        def _():
            rest_load.wait()

            mask_piece(2)
            mask_piece(3)

        @pl.when(t == 1)
        def _():
            @pl.loop(4, n_pieces)
            def _(p):
                mask_piece(p)

            squares[...] = jnp.zeros_like(squares)

        @pl.when(t < n_units - 1)
        def _():
            stage_zero(t + 1)

        @pl.when(t < 2)
        def _():
            hidden_part(t)

        @pl.when(t == 2)
        def _():
            for part in range(2, 4):
                hidden_part(part)

        @pl.when(t == 3)
        def _():
            master_load.wait()
            d_hidden[...] = jnp.zeros_like(d_hidden)

        during(t, 3, data_grad)
        during(t, 4, first_sum)

        @pl.when(jnp.logical_and(t >= n_units + 2, t < n_units + 4))
        def _():
            @pl.loop(0, n_tiles // 2)
            def _(k):
                finish_rows((t - n_units - 2) * (n_tiles // 2) + k)

        during(t, 6, second_sum)
        return carry

    stage_zero(jnp.int32(0))
    lax.fori_loop(0, n_units + 6, step, 0)


def finish(
    gate_v, up_v, master_v, total, squares, dgate_hbm, dup_hbm, new_hbm, new_v, store_sem
):
    n_rows, (n_hidden, width) = gate_v.shape[0], master_v.shape
    parts = 4
    copies = []
    for index, (src, dst) in enumerate(((gate_v, dgate_hbm), (up_v, dup_hbm))):
        for part in range(parts):
            rows = pl.ds(part * (n_rows // parts), n_rows // parts)
            copies.append(
                pltpu.make_async_copy(src.at[rows], dst.at[rows], store_sem.at[index, part])
            )

    def new_store(tile):
        rows = pl.ds(pl.multiple_of(tile * out_tile, out_tile), out_tile)
        return pltpu.make_async_copy(new_v.at[rows], new_hbm.at[rows], store_sem.at[2, tile])

    for copy in copies:
        copy.start()

    @pl.loop(0, n_hidden // out_tile)
    def _(tile):
        rows = pl.ds(pl.multiple_of(tile * out_tile, out_tile), out_tile)
        mean = jnp.sum(squares[rows, :], axis=1, keepdims=True) / width
        scale = learn_rate / jnp.sqrt(mean + rms_eps)
        new_v[rows, :] = master_v[rows, :] - total[rows, :] * scale
        new_store(tile).start()

    for copy in copies:
        copy.wait()

    @pl.loop(0, n_hidden // out_tile)
    def _(tile):
        new_store(tile).wait()


def per_device(grad_out, gate_pre, up_pre, counts, placement, master):
    block, width = grad_out.shape[1:]
    n_rows, n_hidden = gate_pre.shape[1:]
    n_pieces = width // piece
    n_units = n_pieces // 2
    hbm = pl.BlockSpec(memory_space=pl.ANY)
    smem = pl.BlockSpec(memory_space=pltpu.SMEM)
    vmem = pl.BlockSpec(memory_space=pltpu.VMEM)
    dma = pltpu.SemaphoreType.DMA
    pieces = (n_pieces, n_hidden, piece)
    held = pl.pallas_call(
        kernel,
        out_shape=(
            pltpu.VMEM((n_rows, n_hidden), jnp.bfloat16),
            pltpu.VMEM((n_rows, n_hidden), jnp.bfloat16),
            pltpu.VMEM((n_hidden, width), jnp.float32),
            pltpu.VMEM((n_hidden, width), jnp.float32),
            pltpu.VMEM((n_hidden, piece), jnp.float32),
        ),
        in_specs=[hbm, hbm, hbm, smem, smem, hbm],
        out_specs=(vmem,) * 5,
        scratch_shapes=[
            pltpu.VMEM((block, width), jnp.bfloat16),
            pltpu.VMEM((n_pieces, n_rows, piece), jnp.bfloat16),
            pltpu.VMEM((n_hidden, n_rows), jnp.bfloat16),
            pltpu.VMEM((n_rows, n_hidden), jnp.float32),
            pltpu.VMEM((chunk, n_hidden), jnp.bfloat16),
            pltpu.VMEM(pieces, jnp.bfloat16),
            pltpu.VMEM(pieces, jnp.bfloat16),
            pltpu.VMEM(pieces, jnp.bfloat16),
            pltpu.VMEM(pieces, jnp.bfloat16),
            dma((11,)),
            dma((n_units,)),
            dma((n_units, 3)),
            dma((n_pieces - 2 + 2 * last_parts,)),
            dma((n_pieces - 2 + 2 * last_parts,)),
            dma((n_pieces - 2 + 2 * last_parts,)),
            dma((n_pieces - 2 + 2 * last_parts,)),
        ],
        compiler_params=pltpu.CompilerParams(
            collective_id=0, has_side_effects=True, vmem_limit_bytes=40 * 2**20
        ),
    )(grad_out[0], gate_pre[0], up_pre[0], counts, placement, master[0])
    d_gate, d_up, new_master = pl.pallas_call(
        finish,
        out_shape=(
            jax.ShapeDtypeStruct((n_rows, n_hidden), jnp.bfloat16),
            jax.ShapeDtypeStruct((n_rows, n_hidden), jnp.bfloat16),
            jax.ShapeDtypeStruct((n_hidden, width), jnp.float32),
        ),
        in_specs=[vmem] * 5,
        out_specs=(hbm,) * 3,
        scratch_shapes=[pltpu.VMEM((n_hidden, width), jnp.float32), dma((3, 8))],
        compiler_params=pltpu.CompilerParams(vmem_limit_bytes=20 * 2**20),
    )(*held)
    return d_gate[None], d_up[None], new_master[None]


def solution(mesh):
    return jax.shard_map(
        per_device,
        mesh=mesh,
        in_specs=(
            P("expert", "shard", None),
            P("expert", None, "shard"),
            P("expert", None, "shard"),
            P("expert", "shard"),
            P(),
            P("expert", "shard", None),
        ),
        out_specs=(
            P("expert", None, "shard"),
            P("expert", None, "shard"),
            P("expert", "shard", None),
        ),
        check_vma=False,
    )
```
